32 devices in a mesh: seq: 16 (over z, y, x), head: 2 (over core).
Axes of the slice: x: 2, y: 2, z: 4, core: 2. Of those that a mesh axis runs over, the one named last changes fastest.
Arguments:
- block_input: bfloat16 [2048, 2560], P('seq'), may hold values from -6 to 6
- first_gain: bfloat16 [2560], P('seq'), may hold values from 0.5 to 1.5
- gelu_weight: bfloat16 [2560, 2560], P('seq', 'head'), may hold values from -0.125 to 0.125
- scan_weight: bfloat16 [2560, 2560], P('seq', 'head'), may hold values from -0.125 to 0.125
- filter_taps: bfloat16 [4, 10, 256], P(None, 'head', 'seq'), may hold values from -3 to 3
- input_gate: bfloat16 [10, 256, 256], P('head', 'seq'), may hold values from -0.375 to 0.375
- input_bias: bfloat16 [10, 256], P('head', 'seq'), may hold values from -4 to 4
- decay_gate: bfloat16 [10, 256, 256], P('head', 'seq'), may hold values from -0.375 to 0.375
- decay_bias: bfloat16 [10, 256], P('head', 'seq'), may hold values from -4 to 4
- decay_param: bfloat16 [10, 256], P('head', 'seq'), may hold values from -11 to -3
- output_weight: bfloat16 [2560, 2560], P('head', 'seq'), may hold values from -0.125 to 0.125
- second_gain: bfloat16 [2560], P('seq'), may hold values from 0.5 to 1.5
- expand_gate: bfloat16 [2560, 7680], P('seq', 'head'), may hold values from -0.125 to 0.125
- expand_value: bfloat16 [2560, 7680], P('seq', 'head'), may hold values from -0.125 to 0.125
- contract_weight: bfloat16 [7680, 2560], P('head', 'seq'), may hold values from -0.0625 to 0.0625
- output_cotangent: bfloat16 [2048, 2560], P('seq'), may hold values from -6 to 6
Outputs:
- block_output: bfloat16 [2048, 2560], P('seq')
- input_gradient: float32 [2048, 2560], P('seq')
- first_gain_gradient: float32 [2560], P('seq')
- gelu_weight_gradient: float32 [2560, 2560], P('seq', 'head')
- scan_weight_gradient: float32 [2560, 2560], P('seq', 'head')
- filter_taps_gradient: float32 [4, 10, 256], P(None, 'head', 'seq')
- input_gate_gradient: float32 [10, 256, 256], P('head', 'seq')
- input_bias_gradient: float32 [10, 256], P('head', 'seq')
- decay_gate_gradient: float32 [10, 256, 256], P('head', 'seq')
- decay_bias_gradient: float32 [10, 256], P('head', 'seq')
- decay_param_gradient: float32 [10, 256], P('head', 'seq')
- output_weight_gradient: float32 [2560, 2560], P('head', 'seq')
- second_gain_gradient: float32 [2560], P('seq')
- expand_gate_gradient: float32 [2560, 7680], P('seq', 'head')
- expand_value_gradient: float32 [2560, 7680], P('seq', 'head')
- contract_weight_gradient: float32 [7680, 2560], P('head', 'seq')
The draws below stay inside these ranges and needn't reach their ends.
All inputs are finite; a program needn't handle non-finite values.
Results may differ from the reference program's by a relative error of at most 0.017.
Values may be sent and summed in bfloat16 or wider, within the bound.
No kernel may reach another device: no remote copies, remote signals or barrier semaphores. Data moves between devices by JAX's collectives and lax.ppermute only.
A program may use at most 384 MiB of HBM per device.

```python
import jax
import jax.numpy as jnp
from jax import lax

D = 2560
H = 10
B = 256
R = 2560
FF = 7680
K = 4
TOK_DEV = 128
TOKENS = 2048


def strengthened(array, rng, source, target, shards_of, factor):
    def block_of(axis_at):
        return (jnp.arange(array.shape[axis_at]) // (array.shape[axis_at] // shards_of)).reshape((-1,) + (1,) * (array.ndim - 1 - axis_at))

    one_side = jax.random.permutation(rng, shards_of)[block_of(target)]
    other_side = (block_of(target) + shards_of // 2) % shards_of
    return jnp.where((block_of(source) == one_side) | (block_of(source) == other_side), factor * array, array)


def shard_levels(stream_key, extent, split, least, largest):
    def one(dim, parts):
        steps = jax.random.uniform(jax.random.fold_in(jax.random.fold_in(stream_key, 6), dim), (parts,), jnp.float32, least / len(split), largest / len(split))
        return jnp.repeat(jnp.exp(steps), extent[dim] // parts).reshape((-1,) + (1,) * (len(extent) - dim - 1))

    gain = one(*split[0])
    for cut in split[1:]:
        gain = gain * one(*cut)
    return gain


def gaussian(stream_key, extent, deviation, most, split=(), held_as=jnp.bfloat16):
    drawn = jax.random.normal(stream_key, extent, jnp.float32) * deviation
    if len(split) > 0:
        drawn = shard_levels(stream_key, extent, split, -0.22, 0.18) * drawn
    return jnp.clip(drawn, min=-most, max=most).astype(held_as)


def bell_draw_with(stream_key, dims, deviation, bound, cuts, heavy, held_as=jnp.bfloat16):
    entries = deviation * jax.random.normal(stream_key, dims, jnp.float32)
    if cuts:
        entries = entries * shard_levels(stream_key, dims, cuts, -0.22, 0.18)
    return jnp.clip(strengthened(entries, jax.random.fold_in(stream_key, 3), *heavy), -bound, bound).astype(held_as)


def setup_inputs(seed: int = 0) -> dict:
    arg_keys = jax.random.split(jax.random.key(seed), 17)
    return {
        "block_input": bell_draw_with(arg_keys[0], (TOKENS, D), 1.0, 6.0, ((0, 16),), (0, 1, 16, 2.0)),
        "first_gain": jnp.clip(1.0 + 0.1 * jax.random.normal(arg_keys[1], (D,), jnp.float32), 0.5, 1.5).astype(jnp.bfloat16),
        "gelu_weight": gaussian(arg_keys[2], (D, R), D ** -0.5, 0.125, ((0, 16), (1, 2))),
        "scan_weight": gaussian(arg_keys[3], (D, R), D ** -0.5, 0.125, ((0, 16), (1, 2))),
        "filter_taps": gaussian(arg_keys[4], (K, H, B), 0.5, 3.0, ((1, 2), (2, 16))),
        "input_gate": gaussian(arg_keys[5], (H, B, B), B ** -0.5, 0.375, ((0, 2), (1, 16))),
        "input_bias": gaussian(arg_keys[6], (H, B), 1.0, 4.0, ((0, 2), (1, 16))),
        "decay_gate": gaussian(arg_keys[7], (H, B, B), B ** -0.5, 0.375, ((0, 2), (1, 16))),
        "decay_bias": gaussian(arg_keys[8], (H, B), 1.0, 4.0, ((0, 2), (1, 16))),
        "decay_param": jnp.clip(-11.0 + 8.0 * jax.random.uniform(arg_keys[9], (H, B), jnp.float32) ** shard_levels(arg_keys[9], (H, B), ((0, 2), (1, 16)), -0.2, 0.2), -11.0, -3.0).astype(jnp.bfloat16),
        "output_weight": gaussian(arg_keys[10], (R, D), R ** -0.5, 0.125, ((0, 2), (1, 16))),
        "second_gain": jnp.clip(1.0 + 0.1 * jax.random.normal(arg_keys[11], (D,), jnp.float32), 0.5, 1.5).astype(jnp.bfloat16),
        "expand_gate": gaussian(arg_keys[12], (D, FF), D ** -0.5, 0.125, ((0, 16), (1, 2))),
        "expand_value": gaussian(arg_keys[13], (D, FF), D ** -0.5, 0.125, ((0, 16), (1, 2))),
        "contract_weight": gaussian(arg_keys[14], (FF, D), FF ** -0.5, 0.0625, ((0, 2), (1, 16))),
        "output_cotangent": bell_draw_with(arg_keys[15], (TOKENS, D), 1.0, 6.0, ((0, 16),), (0, 1, 16, 2.0)),
    }


EPSILON = 1e-06

@jax.custom_vjp
def low(v):
    return lax.optimization_barrier(v.astype(jnp.bfloat16)).astype(jnp.float32)

@jax.custom_vjp
def low_back(v):
    return v

def low_keep(v):
    return (low(v), None)

def low_pass(kept, grad):
    return (grad,)

def back_keep(v):
    return (v, None)

def back_low(kept, grad):
    return (low(grad),)
low.defvjp(low_keep, low_pass)
low_back.defvjp(back_keep, back_low)

def matmul(left_matrix, right_matrix):
    return jnp.dot(left_matrix, right_matrix, precision=lax.Precision.HIGHEST)

def root_norm(values, gain_row):
    return values * lax.rsqrt(lax.optimization_barrier(jnp.mean(values * values, axis=-1, keepdims=True)) + EPSILON) * gain_row

def blockwise(values, weight_blocks):
    token_count = values.shape[0]
    shaped = values.reshape(token_count, weight_blocks.shape[0], weight_blocks.shape[1])
    return jnp.einsum('thi,hij->thj', shaped, weight_blocks, precision=lax.Precision.HIGHEST).reshape(token_count, -1)

def gating(pre_input, pre_decay, decay_param, filtered):
    input_open = jax.nn.sigmoid(pre_input)
    decay_open = jax.nn.sigmoid(pre_decay)
    log_decay = -8.0 * decay_open * jax.nn.softplus(decay_param)
    decay_rate = jnp.exp(log_decay)
    return (decay_rate, jnp.sqrt(-jnp.expm1(2.0 * log_decay)) * input_open * filtered)

def scan_block(carry_state, element_pair):

    def one_step(running, element):
        running = element[0] * running + element[1]
        return (running, running)
    return lax.scan(one_step, carry_state, element_pair)

def recurrence(decay_rate, update):
    token_count, channels = decay_rate.shape
    blocks = token_count // TOK_DEV
    start_state = jnp.zeros((channels,), jnp.float32)
    _, states = lax.scan(jax.checkpoint(scan_block), start_state, (decay_rate.reshape(blocks, TOK_DEV, channels), update.reshape(blocks, TOK_DEV, channels)))
    return states.reshape(token_count, channels)

def convolve(branch, filter_taps):
    token_count = branch.shape[0]
    tap_rows = filter_taps.reshape(K, R)
    padded = jnp.concatenate([jnp.zeros((K - 1, R), jnp.float32), branch], axis=0)
    filtered = jnp.zeros_like(branch)
    for offset in range(K):
        filtered = filtered + tap_rows[offset] * padded[K - 1 - offset:K - 1 - offset + token_count]
    return filtered

def feed_forward(middle, second_gain, expand_gate, expand_value, contract_weight):

    def one_block(rows_block):
        second = low(root_norm(rows_block, second_gain))
        gate_pre = low_back(matmul(second, expand_gate))
        value_pre = low_back(matmul(second, expand_value))
        hidden = low(jax.nn.gelu(gate_pre) * value_pre)
        return rows_block + low_back(matmul(hidden, contract_weight))
    pieces = middle.reshape(-1, TOK_DEV, D)
    return lax.map(jax.checkpoint(one_block), pieces).reshape(-1, D)

def forward(block_input, first_gain, gelu_weight, scan_weight, filter_taps, input_gate, input_bias, decay_gate, decay_bias, decay_param, output_weight, second_gain, expand_gate, expand_value, contract_weight):
    normed = low(root_norm(block_input, first_gain))
    gelu_pre = low_back(matmul(normed, gelu_weight))
    branch = low_back(matmul(normed, scan_weight))
    filtered = convolve(branch, filter_taps)
    filtered_low = low(filtered)
    pre_input = low_back(blockwise(filtered_low, input_gate)) + input_bias.reshape(-1)
    pre_decay = low_back(blockwise(filtered_low, decay_gate)) + decay_bias.reshape(-1)
    decay_rate, update = gating(pre_input, pre_decay, decay_param.reshape(-1), filtered)
    states = recurrence(decay_rate, update)
    merged = low(states * jax.nn.gelu(gelu_pre))
    middle = block_input + low_back(matmul(merged, output_weight))
    return feed_forward(middle, second_gain, expand_gate, expand_value, contract_weight)

def reference(block_input, first_gain, gelu_weight, scan_weight, filter_taps, input_gate, input_bias, decay_gate, decay_bias, decay_param, output_weight, second_gain, expand_gate, expand_value, contract_weight, output_cotangent):
    inputs = [value.astype(jnp.float32) for value in (block_input, first_gain, gelu_weight, scan_weight, filter_taps, input_gate, input_bias, decay_gate, decay_bias, decay_param, output_weight, second_gain, expand_gate, expand_value, contract_weight)]
    result, pullback = jax.vjp(forward, *inputs)
    gradients = pullback(output_cotangent.astype(jnp.float32))
    return (result.astype(jnp.bfloat16), gradients[0], gradients[1], gradients[2], gradients[3], gradients[4], gradients[5], gradients[6], gradients[7], gradients[8], gradients[9], gradients[10], gradients[11], gradients[12], gradients[13], gradients[14])
```

```python
import functools

import jax
import jax.numpy as jnp
from jax import lax
from jax.experimental import pallas as pl
from jax.experimental.pallas import tpu as pltpu
from jax.sharding import PartitionSpec as P

BF16 = jnp.bfloat16
F32 = jnp.float32
EPSILON = 1e-06
BOTH = ("seq", "head")
LANES = 128
CHUNK = 128
GELU_A = 0.7978845608028654
GELU_B = 0.044715
VMEM_BYTES = 56 * 1024 * 1024


def xor_send(value, mask_first, mask_second=None, allowed=None):
    count = lax.axis_size("seq")
    masks = (mask_first, mask_first if mask_second is None else mask_second)
    pairs = [
        (chip * 2 + core, (chip ^ masks[core]) * 2 + core)
        for chip in range(count)
        for core in range(2)
        if allowed is None or allowed(chip, chip ^ masks[core])
    ]
    return lax.ppermute(value, BOTH, pairs)


def core_swap(value):
    return lax.ppermute(value, "head", [(0, 1), (1, 0)])


def gathered(rows):
    count = lax.axis_size("seq")
    columns = [rows] + [xor_send(rows, 4 * g) for g in range(1, count // 4)]
    own = []
    for block in columns:
        near = xor_send(block, 2, 1)
        own.append(
            jnp.concatenate([block, xor_send(block, 1, 2), near, xor_send(near, 1, 2)], axis=0)
        )
    other = [core_swap(group) for group in own]
    return jnp.concatenate(own + other, axis=0)


def scattered(partial):
    count = lax.axis_size("seq")
    blocks = partial.reshape(count // 4, 4, -1, partial.shape[-1])
    arriving = []
    own = None
    for g in list(range(1, count // 4)) + [0]:
        near = blocks[g, 2] + xor_send(blocks[g, 3].astype(BF16), 1, 2).astype(F32)
        here = blocks[g, 0] + xor_send(blocks[g, 1].astype(BF16), 1, 2).astype(F32)
        here = here + xor_send(near.astype(BF16), 2, 1).astype(F32)
        if g:
            arriving.append(xor_send(here.astype(BF16), 4 * g))
        else:
            own = here
    for more in arriving:
        own = own + more.astype(F32)
    return own


def exchanged(pieces, allowed):
    count = lax.axis_size("seq")
    return jnp.stack([pieces[0]] + [xor_send(pieces[j], j, None, allowed) for j in range(1, count)])


def params(**more):
    return pltpu.CompilerParams(vmem_limit_bytes=VMEM_BYTES, **more)


def picked_body(index, source, target):
    target[...] = source[...]


def picked(blocks, index):
    shape = blocks.shape[1:]
    zeros = (0,) * len(shape)
    return pl.pallas_call(
        picked_body,
        out_shape=jax.ShapeDtypeStruct((index.shape[0],) + shape, blocks.dtype),
        grid_spec=pltpu.PrefetchScalarGridSpec(
            num_scalar_prefetch=1,
            grid=(index.shape[0],),
            in_specs=[pl.BlockSpec((1,) + shape, lambda j, at: (at[j],) + zeros)],
            out_specs=pl.BlockSpec((1,) + shape, lambda j, at: (j,) + zeros),
        ),
        compiler_params=params(),
    )(index, blocks)


def gelu_parts(w):
    inner = jnp.tanh(GELU_A * (w + GELU_B * w * w * w))
    return 0.5 * w * (1.0 + inner), inner


def gelu_slope(w, inner):
    return 0.5 * (1.0 + inner) + 0.5 * w * (1.0 - inner * inner) * GELU_A * (
        1.0 + 3.0 * GELU_B * w * w
    )


def rate_parts(ga, soft_row):
    log_rate = -8.0 * ga * soft_row
    twice = 2.0 * log_rate
    near = -twice * (
        1.0 + twice * (0.5 + twice * (1.0 / 6 + twice * (1.0 / 24 + twice * (1.0 / 120))))
    )
    rate = jnp.exp(log_rate)
    far = 1.0 - jnp.exp(twice)
    return rate, jnp.sqrt(jnp.where(twice > -0.1, near, far))


def filter_kernel(slot, yv, rows, y, vp, c, cb, *, th, taps):
    total = y.shape[0]
    vp[0:8, :] = jnp.zeros((8, LANES), F32)

    def order(b, carry):
        block = yv[pl.ds(pl.multiple_of(slot[b] * th, th), th), :]
        y[pl.ds(pl.multiple_of(b * th, th), th), :] = block[:, :LANES]
        vp[pl.ds(pl.multiple_of(b * th + 8, 8), th), :] = block[:, LANES:]
        return carry

    lax.fori_loop(0, total // th, order, 0)

    def chunk(i, carry):
        start = pl.multiple_of(i * CHUNK, CHUNK)
        window = vp[pl.ds(start, CHUNK + 8), :]
        out = rows[0:1, :] * window[8 : 8 + CHUNK]
        for k in range(1, taps):
            out = out + rows[k : k + 1, :] * window[8 - k : 8 - k + CHUNK]
        c[pl.ds(start, CHUNK), :] = out
        cb[pl.ds(start, CHUNK), :] = out.astype(BF16)
        return carry

    lax.fori_loop(0, total // CHUNK, chunk, 0)


def state_kernel(slot, cbo, cbx, near, far, c, y, rows, gi, ga, hp, ob, a, p, *, th):
    total = y.shape[0]
    length = total // 8
    bias_i, bias_a, soft = rows[0:1, :], rows[1:2, :], rows[2:3, :]

    def chunk(i, carry):
        at = pl.ds(pl.multiple_of(i * CHUNK, CHUNK), CHUNK)
        pre = jnp.dot(cbo[at, :], near[...], preferred_element_type=F32) + jnp.dot(
            cbx[at, :], far[...], preferred_element_type=F32
        )
        open_i = jax.nn.sigmoid(pre[:, :LANES] + bias_i)
        open_a = jax.nn.sigmoid(pre[:, LANES:] + bias_a)
        rate, scale = rate_parts(open_a, soft)
        gi[at, :] = open_i
        ga[at, :] = open_a
        a[at, :] = rate
        hp[pl.ds(pl.multiple_of(i * CHUNK + 8, 8), CHUNK), :] = scale * open_i * c[at, :]
        return carry

    lax.fori_loop(0, total // CHUNK, chunk, 0)

    def step(t, carry):
        h, q = carry
        at = pl.ds(t, 8, stride=length)
        rate = a[at, :]
        h = rate * h + hp[pl.ds(t + 8, 8, stride=length), :]
        q = q * rate
        hp[pl.ds(t + 8, 8, stride=length), :] = h
        p[at, :] = q
        return h, q

    last, product = lax.fori_loop(
        0,
        length,
        step,
        (jnp.zeros((8, LANES), F32), jnp.ones((8, LANES), F32)),
        unroll=8,
    )
    hp[0:8, :] = jnp.zeros((8, LANES), F32)
    entering = [jnp.zeros((1, LANES), F32)]
    for j in range(7):
        entering.append(last[j : j + 1] + product[j : j + 1] * entering[-1])

    per = length // th
    for j in range(8):
        enter = entering[j]

        def finish(i, carry, j=j, enter=enter):
            b = j * per + i
            at = pl.ds(pl.multiple_of(b * th, th), th)
            ahead = pl.ds(pl.multiple_of(b * th + 8, 8), th)
            h = hp[ahead, :] + p[at, :] * enter
            hp[ahead, :] = h
            out, _ = gelu_parts(y[at, :])
            ob[pl.ds(pl.multiple_of(slot[b] * th, th), th), :] = (h * out).astype(BF16)
            return carry

        lax.fori_loop(0, per, finish, 0)


def adjoint_kernel(
    slot, dob, y, hp, gi, ga, c, rows, dy, dpp, dc, sums, lam, a, q, *, th
):
    total = y.shape[0]
    length = total // 8
    soft = rows[2:3, :]

    def order(b, carry):
        at = pl.ds(pl.multiple_of(b * th, th), th)
        there = pl.ds(pl.multiple_of(slot[b] * th, th), th)
        block = dob[there, :]
        w = y[at, :]
        out, inner = gelu_parts(w)
        lam[at, :] = block * out
        h = hp[pl.ds(pl.multiple_of(b * th + 8, 8), th), :]
        dy[there, :] = (block * h * gelu_slope(w, inner)).astype(BF16)
        a[at, :] = jnp.exp(-8.0 * ga[at, :] * soft)
        return carry

    lax.fori_loop(0, total // th, order, 0)

    def step(i, carry):
        later, product = carry
        at = pl.ds(length - 1 - i, 8, stride=length)
        here = lam[at, :] + later
        lam[at, :] = here
        q[at, :] = product
        rate = a[at, :]
        return rate * here, product * rate

    first, product = lax.fori_loop(
        0,
        length,
        step,
        (jnp.zeros((8, LANES), F32), jnp.ones((8, LANES), F32)),
        unroll=8,
    )
    entering = [jnp.zeros((1, LANES), F32)]
    for j in range(7, 0, -1):
        entering.append(first[j : j + 1] + product[j : j + 1] * entering[-1])
    entering = entering[::-1]

    per = length // th
    carry = (jnp.zeros((1, LANES), F32),) * 3
    for j in range(8):
        enter = entering[j]

        def finish(i, carry, j=j, enter=enter):
            b = j * per + i
            start = pl.multiple_of(b * th, th)
            at = pl.ds(start, th)
            state_grad = lam[at, :] + q[at, :] * enter
            before = hp[pl.ds(start, th + 8), :][7 : 7 + th]
            open_i, open_a, filtered = gi[at, :], ga[at, :], c[at, :]
            rate, scale = rate_parts(open_a, soft)
            dla = state_grad * before * rate - state_grad * open_i * filtered * rate * rate / scale
            dpi = state_grad * scale * filtered * open_i * (1.0 - open_i)
            slope = -8.0 * open_a * dla
            dpa = soft * slope * (1.0 - open_a)
            dpp[at, :LANES] = dpi.astype(BF16)
            dpp[at, LANES:] = dpa.astype(BF16)
            dc[at, :] = state_grad * scale * open_i
            return (
                carry[0] + jnp.sum(dpi, axis=0, keepdims=True),
                carry[1] + jnp.sum(dpa, axis=0, keepdims=True),
                carry[2] + jnp.sum(slope, axis=0, keepdims=True),
            )

        carry = lax.fori_loop(0, per, finish, carry)
    sums[...] = jnp.zeros_like(sums)
    for row in range(3):
        sums[row : row + 1, :] = carry[row]


def unfilter_kernel(
    slot, dpo, dpx, near, far, dc, vp, rows, dv, sums, dcp, *, th, taps
):
    total = dc.shape[0]
    last = (((1,), (1,)), ((), ()))
    dcp[total : total + 8, :] = jnp.zeros((8, LANES), F32)

    def chunk(i, carry):
        start = pl.multiple_of(i * CHUNK, CHUNK)
        at = pl.ds(start, CHUNK)
        whole = (
            dc[at, :]
            + lax.dot_general(dpo[at, :], near[...], last, preferred_element_type=F32)
            + lax.dot_general(dpx[at, :], far[...], last, preferred_element_type=F32)
        )
        dcp[at, :] = whole
        window = vp[pl.ds(start, CHUNK + 8), :]
        return tuple(
            carry[k] + jnp.sum(whole * window[8 - k : 8 - k + CHUNK], axis=0, keepdims=True)
            for k in range(taps)
        )

    carry = lax.fori_loop(
        0, total // CHUNK, chunk, tuple(jnp.zeros((1, LANES), F32) for _ in range(taps))
    )
    sums[...] = jnp.zeros_like(sums)
    for k in range(taps):
        sums[k : k + 1, :] = carry[k]

    def order(b, carry):
        window = dcp[pl.ds(pl.multiple_of(b * th, th), th + 8), :]
        out = rows[0:1, :] * window[0:th]
        for k in range(1, taps):
            out = out + rows[k : k + 1, :] * window[k : k + th]
        dv[pl.ds(pl.multiple_of(slot[b] * th, th), th), :] = out.astype(BF16)
        return carry

    lax.fori_loop(0, total // th, order, 0)


def on_chip(kernel, slot, inputs, outs, scratch=()):
    vmem = pl.BlockSpec(memory_space=pltpu.VMEM)
    return pl.pallas_call(
        kernel,
        out_shape=[jax.ShapeDtypeStruct(shape, dtype) for shape, dtype in outs],
        in_specs=[pl.BlockSpec(memory_space=pltpu.SMEM)] + [vmem] * len(inputs),
        out_specs=[vmem] * len(outs),
        scratch_shapes=[pltpu.VMEM(shape, dtype) for shape, dtype in scratch],
        compiler_params=params(),
    )(slot, *inputs)


def dot(left, right, over):
    return lax.dot_general(left, right, (over, ((), ())), preferred_element_type=F32)


def shards(
    block_input,
    first_gain,
    gelu_weight,
    scan_weight,
    filter_taps,
    input_gate,
    input_bias,
    decay_gate,
    decay_bias,
    decay_param,
    output_weight,
    second_gain,
    expand_gate,
    expand_value,
    contract_weight,
    output_cotangent,
):
    count = lax.axis_size("seq")
    chip = lax.axis_index("seq")
    core = lax.axis_index("head")
    slots = jnp.arange(count, dtype=jnp.int32)
    here = chip ^ slots
    th = block_input.shape[0] // 2
    width = block_input.shape[1]
    part = gelu_weight.shape[0]
    taps = filter_taps.shape[0]
    local_blocks, gate_rows, block_width = input_gate.shape
    blocks = 2 * local_blocks
    assert block_width == 2 * LANES and width == part * count
    mine = count * th
    total = 2 * mine

    chip_of = [b * count // blocks for b in range(blocks)]
    assert count >= blocks
    block_of = [chip_of.index(s) if s in chip_of else 0 for s in range(count)]
    gate_chips = frozenset(chip_of)
    hidden = expand_gate.shape[1]
    lanes = LANES * -(-hidden // (count * LANES))
    hidden_chips = hidden // lanes
    assert hidden_chips * lanes == hidden

    number = jnp.arange(2 * count, dtype=jnp.int32)
    relative = chip ^ (number // 2)
    turned = (relative & ~3) | ((relative & 1) << 1) | ((relative >> 1) & 1)
    slot = jnp.where(number % 2 == 0, relative, turned) + jnp.where(
        number % 2 == core, 0, count
    )
    slot = slot.astype(jnp.int32)

    x = lax.dynamic_slice_in_dim(block_input, core * th, th, 0).astype(F32)
    s1 = lax.rsqrt(jnp.mean(x * x, axis=-1, keepdims=True) + EPSILON)
    first = gathered((x * s1).astype(BF16))

    extra = max(16, gate_rows)
    gain1 = first_gain.astype(F32)[:, None]
    mats = jnp.stack(
        [
            (gelu_weight.astype(F32) * gain1).astype(BF16),
            (scan_weight.astype(F32) * gain1).astype(BF16),
            output_weight.T,
        ],
        axis=1,
    ).reshape(part, 3, local_blocks, 2, LANES)
    mats = mats.transpose(3, 2, 0, 1, 4).reshape(2, local_blocks, part, 3 * LANES)
    small = jnp.concatenate(
        [
            filter_taps.transpose(1, 0, 2),
            input_bias[:, None],
            decay_bias[:, None],
            decay_param[:, None],
        ],
        axis=1,
    )
    small = jnp.pad(
        small, ((0, 0), (0, extra - small.shape[1]), (0, LANES - small.shape[2]))
    )
    gates = jnp.stack([input_gate, decay_gate], axis=2).reshape(
        local_blocks, gate_rows, 2, 2, LANES
    )
    gates = jnp.pad(gates, ((0, 0), (0, extra - gate_rows), (0, 0), (0, 0), (0, 0)))
    gates = gates.transpose(3, 0, 1, 2, 4).reshape(2, local_blocks, extra, 2 * LANES)
    gates = jnp.concatenate([gates, jnp.broadcast_to(small, (2,) + small.shape)], axis=-1)
    mats = jnp.concatenate([mats, gates], axis=2)
    kept = lax.dynamic_index_in_dim(mats, core, 0, False)
    given = core_swap(lax.dynamic_index_in_dim(mats, 1 - core, 0, False))
    mats = jnp.concatenate(
        [jnp.where(core == 0, kept, given), jnp.where(core == 0, given, kept)], axis=0
    )
    mats = picked(mats, jnp.asarray(block_of, jnp.int32)[here])
    mats = exchanged(mats, lambda source, target: target in gate_chips)
    mats = picked(mats, here)
    weights = mats[:, :part].reshape(width, 3 * LANES)
    weight_yv, weight_out = weights[:, : 2 * LANES], weights[:, 2 * LANES :]
    gates = mats[:, part : part + gate_rows, : 2 * LANES].reshape(block_width, 2 * LANES)
    small = mats[:, part : part + taps + 3, 2 * LANES : 2 * LANES + gate_rows]
    small = small.transpose(1, 0, 2).reshape(taps + 3, block_width)
    small = lax.dynamic_slice_in_dim(small, core * LANES, LANES, 1).astype(F32)
    tap_rows = jnp.pad(small[:taps], ((0, 8 - taps), (0, 0)))
    param_row = small[taps + 2 :]
    gate_rows_of = jnp.pad(
        jnp.concatenate([small[taps : taps + 2], jax.nn.softplus(param_row)], axis=0),
        ((0, 5), (0, 0)),
    )
    weights_other = core_swap(weights)
    gates_other = core_swap(gates)
    own_half = lambda a: lax.dynamic_slice_in_dim(a, core * LANES, LANES, 0)
    far_half = lambda a: lax.dynamic_slice_in_dim(a, (1 - core) * LANES, LANES, 0)

    gain2 = second_gain.astype(F32)[:, None]
    wide = jnp.stack(
        [
            (expand_gate.astype(F32) * gain2).astype(BF16),
            (expand_value.astype(F32) * gain2).astype(BF16),
            contract_weight.T,
        ],
        axis=1,
    ).reshape(part, 3, hidden_chips, lanes)
    wide = wide.transpose(2, 0, 1, 3).reshape(hidden_chips, part, 3 * lanes)
    wide = picked(wide, jnp.minimum(here, hidden_chips - 1).astype(jnp.int32))
    wide = exchanged(wide, lambda source, target: target < hidden_chips)
    wide = picked(wide, here).reshape(width, 3 * lanes)
    wide_other = core_swap(wide)
    cotangent = lax.dynamic_slice_in_dim(output_cotangent, core * th, th, 0)
    given_out = gathered(cotangent)

    yv = dot(first, weight_yv, ((1,), (0,)))
    token_f32, token_bf16 = ((total, LANES), F32), ((total, LANES), BF16)
    padded = ((total + 8, LANES), F32)
    y, vp, c, cb = on_chip(
        functools.partial(filter_kernel, th=th, taps=taps),
        slot,
        [yv, tap_rows],
        [token_f32, padded, token_f32, token_bf16],
    )
    cb_other = core_swap(cb)
    gate_near, gate_far = own_half(gates), far_half(gates)
    gi, ga, hp, ob = on_chip(
        functools.partial(state_kernel, th=th),
        slot,
        [cb, cb_other, gate_near, gate_far, c, y, gate_rows_of],
        [token_f32, token_f32, padded, token_bf16],
        [token_f32, token_f32],
    )
    merged = jnp.concatenate([ob[:mine], core_swap(ob[mine:])], axis=1)
    out_both = jnp.concatenate([weight_out, weights_other[:, 2 * LANES :]], axis=1)
    r = x + scattered(dot(merged, out_both, ((1,), (1,))))

    s2 = lax.rsqrt(jnp.mean(r * r, axis=-1, keepdims=True) + EPSILON)
    second = gathered((r * s2).astype(BF16))
    weight_ge, weight_c = wide[:, : 2 * lanes], wide[:, 2 * lanes :]
    ge = dot(second, weight_ge, ((1,), (0,)))
    dz = dot(given_out, weight_c, ((1,), (0,)))
    g, e = ge[:, :lanes], ge[:, lanes:]
    act, inner = gelu_parts(g)
    zb = (act * e).astype(BF16)
    dgate = (dz * e * gelu_slope(g, inner)).astype(BF16)
    dvalue = (dz * act).astype(BF16)
    dge = jnp.concatenate([dgate, dvalue], axis=1)
    dge_both = jnp.concatenate([dge[:mine], core_swap(dge[mine:])], axis=1)
    ge_both = jnp.concatenate([weight_ge, wide_other[:, : 2 * lanes]], axis=1)
    back2 = scattered(dot(dge_both, ge_both, ((1,), (1,))))
    dr = (
        cotangent.astype(F32)
        + s2 * back2
        - r * (s2 * s2 * s2) * jnp.mean(back2 * r, axis=-1, keepdims=True)
    )
    zb_both = jnp.concatenate([zb[:mine], core_swap(zb[mine:])], axis=1)
    c_both = jnp.concatenate([weight_c, wide_other[:, 2 * lanes :]], axis=1)
    out_half = (r + scattered(dot(zb_both, c_both, ((1,), (1,))))).astype(BF16)

    wide_grad = jnp.concatenate(
        [dot(second, dge, ((0,), (0,))), dot(given_out, zb, ((0,), (0,)))], axis=1
    ).astype(BF16)
    wide_grad = picked(wide_grad.reshape(count, part, 3 * lanes), here)
    wide_grad = exchanged(wide_grad, lambda source, target: source < hidden_chips)
    wide_grad = picked(wide_grad, here)[:hidden_chips].astype(F32)
    wide_grad = wide_grad.transpose(1, 0, 2).reshape(part, hidden_chips, 3, lanes)
    gate_hat, value_hat, contract_t = (wide_grad[:, :, i].reshape(part, hidden) for i in range(3))
    gain2_part = jnp.sum(
        gate_hat * expand_gate.astype(F32) + value_hat * expand_value.astype(F32), axis=1
    )

    dq = gathered(dr.astype(BF16))
    dob = dot(dq, weight_out, ((1,), (0,)))
    dy, dpp, dc, sums = on_chip(
        functools.partial(adjoint_kernel, th=th),
        slot,
        [dob, y, hp, gi, ga, c, gate_rows_of],
        [token_bf16, ((total, 2 * LANES), BF16), token_f32, ((8, LANES), F32)],
        [token_f32, token_f32, token_f32],
    )
    dpp_other = core_swap(dpp)
    dv, tap_sums = on_chip(
        functools.partial(unfilter_kernel, th=th, taps=taps),
        slot,
        [dpp, dpp_other, gate_near, own_half(gates_other), dc, vp, tap_rows],
        [token_bf16, ((8, LANES), F32)],
        [padded],
    )
    dyv = jnp.concatenate([dy, dv], axis=1)
    dyv_both = jnp.concatenate([dyv[:mine], core_swap(dyv[mine:])], axis=1)
    yv_both = jnp.concatenate([weight_yv, weights_other[:, : 2 * LANES]], axis=1)
    back1 = scattered(dot(dyv_both, yv_both, ((1,), (1,))))
    in_half = dr + s1 * back1 - x * (s1 * s1 * s1) * jnp.mean(back1 * x, axis=-1, keepdims=True)

    yv_grad = dot(first, dyv, ((0,), (0,)))
    out_grad = dot(dq, ob, ((0,), (0,)))
    weight_grad = jnp.concatenate([yv_grad, out_grad], axis=1).astype(BF16)
    weight_grad = weight_grad.reshape(count, part, 3 * LANES)
    own_grad, far_grad = dot(cb, dpp, ((0,), (0,))), dot(cb_other, dpp, ((0,), (0,)))
    gate_grad = jnp.concatenate(
        [jnp.where(core == 0, own_grad, far_grad), jnp.where(core == 0, far_grad, own_grad)], axis=0
    )
    gate_grad = jnp.pad(
        gate_grad.reshape(count, gate_rows, 2 * LANES), ((0, 0), (0, extra - gate_rows), (0, 0))
    )
    small_grad = jnp.concatenate(
        [tap_sums[:taps], sums[:2], sums[2:3] * jax.nn.sigmoid(param_row)], axis=0
    )
    small_grad = jnp.concatenate(
        [
            jnp.where(core == 0, small_grad, 0.0),
            jnp.where(core == 0, 0.0, small_grad),
        ],
        axis=1,
    )
    small_grad = small_grad.reshape(taps + 3, count, gate_rows).transpose(1, 0, 2)
    small_grad = jnp.pad(
        small_grad, ((0, 0), (0, extra - taps - 3), (0, LANES - gate_rows))
    )
    gate_grad = jnp.concatenate([gate_grad, small_grad], axis=-1).astype(BF16)
    weight_grad = jnp.concatenate([weight_grad, gate_grad], axis=1)
    weight_grad = picked(weight_grad, here)
    weight_grad = exchanged(weight_grad, lambda source, target: source in gate_chips)
    weight_grad = picked(weight_grad, (jnp.asarray(chip_of, jnp.int32) ^ chip).astype(jnp.int32))
    kept = lax.dynamic_slice_in_dim(weight_grad, core * local_blocks, local_blocks, 0)
    given = lax.dynamic_slice_in_dim(weight_grad, (1 - core) * local_blocks, local_blocks, 0)
    given = core_swap(given)
    halves = jnp.stack(
        [jnp.where(core == 0, kept, given), jnp.where(core == 0, given, kept)], axis=0
    ).astype(F32)
    mats_grad = halves[:, :, :part].reshape(2, local_blocks, part, 3, LANES)
    mats_grad = mats_grad.transpose(3, 2, 1, 0, 4).reshape(3, part, local_blocks * block_width)
    gates_grad = halves[:, :, part : part + gate_rows, : 2 * LANES]
    gates_grad = gates_grad.reshape(2, local_blocks, gate_rows, 2, LANES)
    gates_grad = gates_grad.transpose(3, 1, 2, 0, 4).reshape(
        2, local_blocks, gate_rows, block_width
    )
    small_sum = halves[0, :, part:, 2 * LANES :] + halves[1, :, part:, 2 * LANES :]
    small_sum = small_sum[:, : taps + 3, :gate_rows].transpose(1, 0, 2)
    gain1_part = jnp.sum(
        mats_grad[0] * gelu_weight.astype(F32) + mats_grad[1] * scan_weight.astype(F32), axis=1
    )

    gain_parts = jnp.stack([gain1_part, gain2_part])
    gain_grads = gain_parts + core_swap(gain_parts)

    def both_halves(half):
        swapped = core_swap(half)
        return jnp.concatenate(
            [jnp.where(core == 0, half, swapped), jnp.where(core == 0, swapped, half)], axis=0
        )

    return (
        both_halves(out_half),
        both_halves(in_half),
        gain_grads[0],
        mats_grad[0] * gain1,
        mats_grad[1] * gain1,
        small_sum[:taps],
        gates_grad[0],
        small_sum[taps],
        gates_grad[1],
        small_sum[taps + 1],
        small_sum[taps + 2],
        mats_grad[2].T,
        gain_grads[1],
        gate_hat * gain2,
        value_hat * gain2,
        contract_t.T,
    )


def solution(mesh):
    in_specs = (
        P("seq", None),
        P("seq"),
        P("seq", "head"),
        P("seq", "head"),
        P(None, "head", "seq"),
        P("head", "seq", None),
        P("head", "seq"),
        P("head", "seq", None),
        P("head", "seq"),
        P("head", "seq"),
        P("head", "seq"),
        P("seq"),
        P("seq", "head"),
        P("seq", "head"),
        P("head", "seq"),
        P("seq", None),
    )
    out_specs = (
        P("seq", None),
        P("seq", None),
        P("seq"),
        P("seq", "head"),
        P("seq", "head"),
        P(None, "head", "seq"),
        P("head", "seq", None),
        P("head", "seq"),
        P("head", "seq", None),
        P("head", "seq"),
        P("head", "seq"),
        P("head", "seq"),
        P("seq"),
        P("seq", "head"),
        P("seq", "head"),
        P("head", "seq"),
    )
    return jax.shard_map(shards, mesh=mesh, in_specs=in_specs, out_specs=out_specs, check_vma=False)
```

```python
import functools

import jax
import jax.numpy as jnp
from jax import lax
from jax.experimental import pallas as pl
from jax.experimental.pallas import tpu as pltpu
from jax.sharding import PartitionSpec as P

BF16 = jnp.bfloat16
F32 = jnp.float32
EPSILON = 1e-06
BOTH = ("seq", "head")
LANES = 128
CHUNK = 128
GELU_A = 0.7978845608028654
GELU_B = 0.044715
VMEM_BYTES = 56 * 1024 * 1024


def xor_send(value, mask_first, mask_second=None, allowed=None):
    count = lax.axis_size("seq")
    masks = (mask_first, mask_first if mask_second is None else mask_second)
    pairs = [
        (chip * 2 + core, (chip ^ masks[core]) * 2 + core)
        for chip in range(count)
        for core in range(2)
        if allowed is None or allowed(chip, chip ^ masks[core])
    ]
    return lax.ppermute(value, BOTH, pairs)


def core_swap(value):
    return lax.ppermute(value, "head", [(0, 1), (1, 0)])


def gathered(rows):
    count = lax.axis_size("seq")
    columns = [rows] + [xor_send(rows, 4 * g) for g in range(1, count // 4)]
    own = []
    for block in columns:
        pair = jnp.concatenate([block, xor_send(block, 2, 1)], axis=0)
        own.append(jnp.concatenate([pair, xor_send(pair, 1, 2)], axis=0))
    return own + [core_swap(group) for group in own]


def scattered(*products):
    count = lax.axis_size("seq") // 4
    rows = products[0][0][0].shape[0] // 4
    parts = len(products)

    def sent(arrays, *masks):
        moved = xor_send(jnp.concatenate([a.astype(BF16) for a in arrays]), *masks)
        return [a.astype(F32) for a in jnp.split(moved, parts)]

    own = None
    arriving = []
    for g in list(range(1, count)) + [0]:
        sums = [dot(groups[g], right, ((1,), (1,))).astype(BF16) for groups, right in products]
        more = sent([a[2 * rows :] for a in sums], 1, 2)
        sums = [a[: 2 * rows].astype(F32) + b for a, b in zip(sums, more)]
        more = sent([a[rows:] for a in sums], 2, 1)
        sums = [a[:rows] + b for a, b in zip(sums, more)]
        if g:
            arriving.append(sent(sums, 4 * g))
        else:
            own = sums
    for more in arriving:
        own = [a + b for a, b in zip(own, more)]
    return own


def grouped(rows):
    half = rows.shape[0] // 2
    both = jnp.concatenate([rows[:half], core_swap(rows[half:])], axis=1)
    return list(both.reshape(lax.axis_size("seq") // 4, -1, both.shape[1]))


def after(value, *others):
    return lax.optimization_barrier((value,) + others)[0]


def all_to_all(pieces):
    return lax.all_to_all(pieces, "seq", 0, 0, tiled=True)


def params(**more):
    return pltpu.CompilerParams(vmem_limit_bytes=VMEM_BYTES, **more)


def pack_wide(gain, gate, value, contract, out, *, chips):
    lanes = gate.shape[1]
    live = pl.program_id(0) < chips
    scale = jnp.where(live, gain[...], 0.0)
    out[0, :, :lanes] = (gate[...].astype(F32) * scale).astype(BF16)
    out[0, :, lanes : 2 * lanes] = (value[...].astype(F32) * scale).astype(BF16)
    out[0, :, 2 * lanes :] = jnp.where(live, contract[...].astype(F32), 0.0).astype(BF16)


def packed_wide(gain, gate, value, contract, count, lanes):
    part, hidden = gate.shape
    chips = hidden // lanes
    column = pl.BlockSpec((part, lanes), lambda j: (0, jnp.minimum(j, chips - 1)))
    return pl.pallas_call(
        functools.partial(pack_wide, chips=chips),
        out_shape=jax.ShapeDtypeStruct((count, part, 3 * lanes), BF16),
        grid=(count,),
        in_specs=[
            pl.BlockSpec((part, 1), lambda j: (0, 0)),
            column,
            column,
            column,
        ],
        out_specs=pl.BlockSpec((1, part, 3 * lanes), lambda j: (j, 0, 0)),
        compiler_params=params(),
    )(gain, gate, value, contract)


def unpack_wide(grads, gain, gate, value, gate_out, value_out, contract_out, sums):
    lanes = gate.shape[1]
    gate_hat = grads[0, :, :lanes].astype(F32)
    value_hat = grads[0, :, lanes : 2 * lanes].astype(F32)
    gate_out[...] = gate_hat * gain[...]
    value_out[...] = value_hat * gain[...]
    contract_out[...] = grads[0, :, 2 * lanes :].astype(F32)
    both = gate_hat * gate[...].astype(F32) + value_hat * value[...].astype(F32)

    @pl.when(pl.program_id(0) == 0)
    def _():
        sums[...] = jnp.zeros_like(sums)

    total = both[:, :LANES]
    for start in range(LANES, lanes, LANES):
        total = total + both[:, start : start + LANES]
    sums[...] += total


def unpacked_wide(grads, gain, gate, value, lanes):
    part, hidden = gate.shape
    column = pl.BlockSpec((part, lanes), lambda j: (0, j))
    return pl.pallas_call(
        unpack_wide,
        out_shape=[
            jax.ShapeDtypeStruct((part, hidden), F32),
            jax.ShapeDtypeStruct((part, hidden), F32),
            jax.ShapeDtypeStruct((part, hidden), F32),
            jax.ShapeDtypeStruct((part, LANES), F32),
        ],
        grid=(hidden // lanes,),
        in_specs=[
            pl.BlockSpec((1, part, 3 * lanes), lambda j: (j, 0, 0)),
            pl.BlockSpec((part, 1), lambda j: (0, 0)),
            column,
            column,
        ],
        out_specs=[
            column,
            column,
            column,
            pl.BlockSpec((part, LANES), lambda j: (0, 0)),
        ],
        compiler_params=params(),
    )(grads, gain, gate, value)


def pack_narrow(gain, gelu, scan, output, in_gate, de_gate, small, out):
    extra = small.shape[1]
    out[0, 0, :extra, :LANES] = in_gate[0]
    out[0, 0, :extra, LANES : 2 * LANES] = de_gate[0]
    out[0, 0, :extra, 2 * LANES :] = small[0]
    out[0, 0, extra:, :LANES] = (gelu[...].astype(F32) * gain[...]).astype(BF16)
    out[0, 0, extra:, LANES : 2 * LANES] = (scan[...].astype(F32) * gain[...]).astype(BF16)
    out[0, 0, extra:, 2 * LANES :] = output[...]


def packed_narrow(gain, gelu, scan, output, in_gate, de_gate, small):
    part = gelu.shape[0]
    local_blocks, extra = small.shape[:2]
    column = pl.BlockSpec((part, LANES), lambda h, b: (0, 2 * b + h))
    gate = pl.BlockSpec((1, extra, LANES), lambda h, b: (b, 0, h))
    return pl.pallas_call(
        pack_narrow,
        out_shape=jax.ShapeDtypeStruct((2, local_blocks, extra + part, 3 * LANES), BF16),
        grid=(2, local_blocks),
        in_specs=[
            pl.BlockSpec((part, 1), lambda h, b: (0, 0)),
            column,
            column,
            column,
            gate,
            gate,
            pl.BlockSpec((1, extra, LANES), lambda h, b: (b, 0, 0)),
        ],
        out_specs=pl.BlockSpec((1, 1, extra + part, 3 * LANES), lambda h, b: (h, b, 0, 0)),
        compiler_params=params(),
    )(gain, gelu, scan, output, in_gate, de_gate, small)


def unpack_narrow(
    grads, gain, gelu, scan, gelu_out, scan_out, output_out, in_out, de_out, sums, *, extra
):
    gelu_hat = grads[0, 0, extra:, :LANES].astype(F32)
    scan_hat = grads[0, 0, extra:, LANES : 2 * LANES].astype(F32)
    gelu_out[...] = gelu_hat * gain[...]
    scan_out[...] = scan_hat * gain[...]
    output_out[...] = grads[0, 0, extra:, 2 * LANES :].astype(F32)
    rows = in_out.shape[1]
    in_out[0] = grads[0, 0, :extra, :LANES].astype(F32)[:rows]
    de_out[0] = grads[0, 0, :extra, LANES : 2 * LANES].astype(F32)[:rows]

    @pl.when((pl.program_id(0) == 0) & (pl.program_id(1) == 0))
    def _():
        sums[...] = jnp.zeros_like(sums)

    sums[...] += gelu_hat * gelu[...].astype(F32) + scan_hat * scan[...].astype(F32)


def unpacked_narrow(grads, gain, gelu, scan, gate_rows):
    part, width = gelu.shape
    local_blocks = grads.shape[1]
    extra = grads.shape[2] - part
    column = pl.BlockSpec((part, LANES), lambda h, b: (0, 2 * b + h))
    gate = pl.BlockSpec((1, gate_rows, LANES), lambda h, b: (b, 0, h))
    return pl.pallas_call(
        functools.partial(unpack_narrow, extra=extra),
        out_shape=[
            jax.ShapeDtypeStruct((part, width), F32),
            jax.ShapeDtypeStruct((part, width), F32),
            jax.ShapeDtypeStruct((part, width), F32),
            jax.ShapeDtypeStruct((local_blocks, gate_rows, 2 * LANES), F32),
            jax.ShapeDtypeStruct((local_blocks, gate_rows, 2 * LANES), F32),
            jax.ShapeDtypeStruct((part, LANES), F32),
        ],
        grid=(2, local_blocks),
        in_specs=[
            pl.BlockSpec((1, 1, extra + part, 3 * LANES), lambda h, b: (h, b, 0, 0)),
            pl.BlockSpec((part, 1), lambda h, b: (0, 0)),
            column,
            column,
        ],
        out_specs=[
            column,
            column,
            column,
            gate,
            gate,
            pl.BlockSpec((part, LANES), lambda h, b: (0, 0)),
        ],
        compiler_params=params(),
    )(grads, gain, gelu, scan)


def gelu_parts(w):
    inner = jnp.tanh(GELU_A * (w + GELU_B * w * w * w))
    return 0.5 * w * (1.0 + inner), inner


def gelu_slope(w, inner):
    return 0.5 * (1.0 + inner) + 0.5 * w * (1.0 - inner * inner) * GELU_A * (
        1.0 + 3.0 * GELU_B * w * w
    )


def rate_parts(ga, soft_row):
    log_rate = -8.0 * ga * soft_row
    twice = 2.0 * log_rate
    near = -twice * (
        1.0 + twice * (0.5 + twice * (1.0 / 6 + twice * (1.0 / 24 + twice * (1.0 / 120))))
    )
    rate = jnp.exp(log_rate)
    far = 1.0 - jnp.exp(twice)
    return rate, jnp.sqrt(jnp.where(twice > -0.1, near, far))


def filter_kernel(slot, yv, rows, y, vp, c, cb, *, th, taps):
    total = y.shape[0]
    vp[0:8, :] = jnp.zeros((8, LANES), F32)

    def order(b, carry):
        block = yv[pl.ds(pl.multiple_of(slot[b] * th, th), th), :]
        y[pl.ds(pl.multiple_of(b * th, th), th), :] = block[:, :LANES]
        vp[pl.ds(pl.multiple_of(b * th + 8, 8), th), :] = block[:, LANES:]
        return carry

    lax.fori_loop(0, total // th, order, 0)

    def chunk(i, carry):
        start = pl.multiple_of(i * CHUNK, CHUNK)
        window = vp[pl.ds(start, CHUNK + 8), :]
        out = rows[0:1, :] * window[8 : 8 + CHUNK]
        for k in range(1, taps):
            out = out + rows[k : k + 1, :] * window[8 - k : 8 - k + CHUNK]
        c[pl.ds(start, CHUNK), :] = out
        cb[pl.ds(start, CHUNK), :] = out.astype(BF16)
        return carry

    lax.fori_loop(0, total // CHUNK, chunk, 0)


def state_kernel(slot, cbo, cbx, near, far, c, y, rows, gi, ga, hp, ob, a, p, *, th):
    total = y.shape[0]
    length = total // 8
    bias_i, bias_a, soft = rows[0:1, :], rows[1:2, :], rows[2:3, :]

    def chunk(i, carry):
        at = pl.ds(pl.multiple_of(i * CHUNK, CHUNK), CHUNK)
        pre = jnp.dot(cbo[at, :], near[...], preferred_element_type=F32) + jnp.dot(
            cbx[at, :], far[...], preferred_element_type=F32
        )
        open_i = jax.nn.sigmoid(pre[:, :LANES] + bias_i)
        open_a = jax.nn.sigmoid(pre[:, LANES:] + bias_a)
        rate, scale = rate_parts(open_a, soft)
        gi[at, :] = open_i
        ga[at, :] = open_a
        a[at, :] = rate
        hp[pl.ds(pl.multiple_of(i * CHUNK + 8, 8), CHUNK), :] = scale * open_i * c[at, :]
        return carry

    lax.fori_loop(0, total // CHUNK, chunk, 0)

    def step(t, carry):
        h, q = carry
        at = pl.ds(t, 8, stride=length)
        rate = a[at, :]
        h = rate * h + hp[pl.ds(t + 8, 8, stride=length), :]
        q = q * rate
        hp[pl.ds(t + 8, 8, stride=length), :] = h
        p[at, :] = q
        return h, q

    last, product = lax.fori_loop(
        0,
        length,
        step,
        (jnp.zeros((8, LANES), F32), jnp.ones((8, LANES), F32)),
        unroll=8,
    )
    hp[0:8, :] = jnp.zeros((8, LANES), F32)
    entering = [jnp.zeros((1, LANES), F32)]
    for j in range(7):
        entering.append(last[j : j + 1] + product[j : j + 1] * entering[-1])

    per = length // th
    for j in range(8):
        enter = entering[j]

        def finish(i, carry, j=j, enter=enter):
            b = j * per + i
            at = pl.ds(pl.multiple_of(b * th, th), th)
            ahead = pl.ds(pl.multiple_of(b * th + 8, 8), th)
            h = hp[ahead, :] + p[at, :] * enter
            hp[ahead, :] = h
            out, _ = gelu_parts(y[at, :])
            ob[pl.ds(pl.multiple_of(slot[b] * th, th), th), :] = (h * out).astype(BF16)
            return carry

        lax.fori_loop(0, per, finish, 0)


def adjoint_kernel(
    slot, dob, y, hp, gi, ga, c, rows, dy, dpp, dc, sums, lam, a, q, *, th
):
    total = y.shape[0]
    length = total // 8
    soft = rows[2:3, :]

    def order(b, carry):
        at = pl.ds(pl.multiple_of(b * th, th), th)
        there = pl.ds(pl.multiple_of(slot[b] * th, th), th)
        block = dob[there, :]
        w = y[at, :]
        out, inner = gelu_parts(w)
        lam[at, :] = block * out
        h = hp[pl.ds(pl.multiple_of(b * th + 8, 8), th), :]
        dy[there, :] = (block * h * gelu_slope(w, inner)).astype(BF16)
        a[at, :] = jnp.exp(-8.0 * ga[at, :] * soft)
        return carry

    lax.fori_loop(0, total // th, order, 0)

    def step(i, carry):
        later, product = carry
        at = pl.ds(length - 1 - i, 8, stride=length)
        here = lam[at, :] + later
        lam[at, :] = here
        q[at, :] = product
        rate = a[at, :]
        return rate * here, product * rate

    first, product = lax.fori_loop(
        0,
        length,
        step,
        (jnp.zeros((8, LANES), F32), jnp.ones((8, LANES), F32)),
        unroll=8,
    )
    entering = [jnp.zeros((1, LANES), F32)]
    for j in range(7, 0, -1):
        entering.append(first[j : j + 1] + product[j : j + 1] * entering[-1])
    entering = entering[::-1]

    per = length // th
    carry = (jnp.zeros((1, LANES), F32),) * 3
    for j in range(8):
        enter = entering[j]

        def finish(i, carry, j=j, enter=enter):
            b = j * per + i
            start = pl.multiple_of(b * th, th)
            at = pl.ds(start, th)
            state_grad = lam[at, :] + q[at, :] * enter
            before = hp[pl.ds(start, th + 8), :][7 : 7 + th]
            open_i, open_a, filtered = gi[at, :], ga[at, :], c[at, :]
            rate, scale = rate_parts(open_a, soft)
            dla = state_grad * before * rate - state_grad * open_i * filtered * rate * rate / scale
            dpi = state_grad * scale * filtered * open_i * (1.0 - open_i)
            slope = -8.0 * open_a * dla
            dpa = soft * slope * (1.0 - open_a)
            dpp[at, :LANES] = dpi.astype(BF16)
            dpp[at, LANES:] = dpa.astype(BF16)
            dc[at, :] = state_grad * scale * open_i
            return (
                carry[0] + jnp.sum(dpi, axis=0, keepdims=True),
                carry[1] + jnp.sum(dpa, axis=0, keepdims=True),
                carry[2] + jnp.sum(slope, axis=0, keepdims=True),
            )

        carry = lax.fori_loop(0, per, finish, carry)
    sums[...] = jnp.zeros_like(sums)
    for row in range(3):
        sums[row : row + 1, :] = carry[row]


def unfilter_kernel(
    slot, dpo, dpx, near, far, dc, vp, rows, dv, sums, dcp, *, th, taps
):
    total = dc.shape[0]
    last = (((1,), (1,)), ((), ()))
    dcp[total : total + 8, :] = jnp.zeros((8, LANES), F32)

    def chunk(i, carry):
        start = pl.multiple_of(i * CHUNK, CHUNK)
        at = pl.ds(start, CHUNK)
        whole = (
            dc[at, :]
            + lax.dot_general(dpo[at, :], near[...], last, preferred_element_type=F32)
            + lax.dot_general(dpx[at, :], far[...], last, preferred_element_type=F32)
        )
        dcp[at, :] = whole
        window = vp[pl.ds(start, CHUNK + 8), :]
        return tuple(
            carry[k] + jnp.sum(whole * window[8 - k : 8 - k + CHUNK], axis=0, keepdims=True)
            for k in range(taps)
        )

    carry = lax.fori_loop(
        0, total // CHUNK, chunk, tuple(jnp.zeros((1, LANES), F32) for _ in range(taps))
    )
    sums[...] = jnp.zeros_like(sums)
    for k in range(taps):
        sums[k : k + 1, :] = carry[k]

    def order(b, carry):
        window = dcp[pl.ds(pl.multiple_of(b * th, th), th + 8), :]
        out = rows[0:1, :] * window[0:th]
        for k in range(1, taps):
            out = out + rows[k : k + 1, :] * window[k : k + th]
        dv[pl.ds(pl.multiple_of(slot[b] * th, th), th), :] = out.astype(BF16)
        return carry

    lax.fori_loop(0, total // th, order, 0)


def feed_kernel(slot, ge, dz, zb, dge, *, th):
    lanes = dz.shape[1]

    def block(b, carry):
        at = pl.ds(pl.multiple_of(b * th, th), th)
        g, e, d = ge[at, :lanes], ge[at, lanes:], dz[at, :]
        act, inner = gelu_parts(g)
        zb[at, :] = (act * e).astype(BF16)
        dge[at, :lanes] = (d * e * gelu_slope(g, inner)).astype(BF16)
        dge[at, lanes:] = (d * act).astype(BF16)
        return carry

    lax.fori_loop(0, dz.shape[0] // th, block, 0)


def on_chip(kernel, slot, inputs, outs, scratch=()):
    vmem = pl.BlockSpec(memory_space=pltpu.VMEM)
    return pl.pallas_call(
        kernel,
        out_shape=[jax.ShapeDtypeStruct(shape, dtype) for shape, dtype in outs],
        in_specs=[pl.BlockSpec(memory_space=pltpu.SMEM)] + [vmem] * len(inputs),
        out_specs=[vmem] * len(outs),
        scratch_shapes=[pltpu.VMEM(shape, dtype) for shape, dtype in scratch],
        compiler_params=params(),
    )(slot, *inputs)


def dot(left, right, over):
    return lax.dot_general(left, right, (over, ((), ())), preferred_element_type=F32)


def shards(
    block_input,
    first_gain,
    gelu_weight,
    scan_weight,
    filter_taps,
    input_gate,
    input_bias,
    decay_gate,
    decay_bias,
    decay_param,
    output_weight,
    second_gain,
    expand_gate,
    expand_value,
    contract_weight,
    output_cotangent,
):
    count = lax.axis_size("seq")
    chip = lax.axis_index("seq")
    core = lax.axis_index("head")
    th = block_input.shape[0] // 2
    width = block_input.shape[1]
    part = gelu_weight.shape[0]
    taps = filter_taps.shape[0]
    local_blocks, gate_rows, block_width = input_gate.shape
    blocks = 2 * local_blocks
    assert block_width == 2 * LANES and width == part * count
    mine = count * th
    total = 2 * mine

    chip_of = [b * count // blocks for b in range(blocks)]
    assert count >= blocks
    block_of = [chip_of.index(s) if s in chip_of else 0 for s in range(count)]
    gate_chips = frozenset(chip_of)
    hidden = expand_gate.shape[1]
    lanes = LANES * -(-hidden // (count * LANES))
    hidden_chips = hidden // lanes
    assert hidden_chips * lanes == hidden

    number = jnp.arange(2 * count, dtype=jnp.int32)
    turn = lambda a: (a & ~3) | ((a & 1) << 1) | ((a >> 1) & 1)
    relative = chip ^ (number // 2)
    slot = jnp.where(number % 2 == 0, turn(relative), relative) + jnp.where(
        number % 2 == core, 0, count
    )
    slot = slot.astype(jnp.int32)
    x = lax.dynamic_slice_in_dim(block_input, core * th, th, 0).astype(F32)
    s1 = lax.rsqrt(jnp.mean(x * x, axis=-1, keepdims=True) + EPSILON)
    cotangent = lax.dynamic_slice_in_dim(output_cotangent, core * th, th, 0)
    both = gathered(jnp.concatenate([(x * s1).astype(BF16), cotangent], axis=0))
    both = [piece.reshape(4, 2, th, width) for piece in both]
    first = [piece[:, 0].reshape(4 * th, width) for piece in both]
    given_out = jnp.concatenate([piece[:, 1].reshape(4 * th, width) for piece in both])

    extra = max(16, gate_rows)
    more_rows = ((0, 0), (0, extra - gate_rows), (0, 0))
    gain1 = first_gain.astype(F32)[:, None]
    small = jnp.concatenate(
        [
            filter_taps.transpose(1, 0, 2),
            input_bias[:, None],
            decay_bias[:, None],
            decay_param[:, None],
        ],
        axis=1,
    )
    small = jnp.pad(
        small, ((0, 0), (0, extra - small.shape[1]), (0, LANES - small.shape[2]))
    )
    mats = packed_narrow(
        gain1,
        gelu_weight,
        scan_weight,
        output_weight.T,
        jnp.pad(input_gate, more_rows),
        jnp.pad(decay_gate, more_rows),
        small,
    )
    kept = lax.dynamic_index_in_dim(mats, core, 0, False)
    given = core_swap(lax.dynamic_index_in_dim(mats, 1 - core, 0, False))
    halves = [jnp.where(core == 0, kept, given), jnp.where(core == 0, given, kept)]
    nothing = jnp.zeros_like(kept[0])
    mats = jnp.stack(
        [
            halves[block_of[c] // local_blocks][block_of[c] % local_blocks]
            if c in gate_chips
            else nothing
            for c in range(count)
        ]
    )
    mats = all_to_all(mats)
    weights = mats[:, extra:].reshape(width, 3 * LANES)
    weight_yv, weight_out = weights[:, : 2 * LANES], weights[:, 2 * LANES :]
    gates = mats[:, :gate_rows, : 2 * LANES].reshape(block_width, 2 * LANES)
    small = mats[:, : taps + 3, 2 * LANES : 2 * LANES + gate_rows]
    small = small.transpose(1, 0, 2).reshape(taps + 3, block_width)
    small = lax.dynamic_slice_in_dim(small, core * LANES, LANES, 1).astype(F32)
    tap_rows = jnp.pad(small[:taps], ((0, 8 - taps), (0, 0)))
    param_row = small[taps + 2 :]
    gate_rows_of = jnp.pad(
        jnp.concatenate([small[taps : taps + 2], jax.nn.softplus(param_row)], axis=0),
        ((0, 5), (0, 0)),
    )
    weights_other = core_swap(weights)
    gates_other = core_swap(gates)
    own_half = lambda a: lax.dynamic_slice_in_dim(a, core * LANES, LANES, 0)
    far_half = lambda a: lax.dynamic_slice_in_dim(a, (1 - core) * LANES, LANES, 0)

    gain2 = second_gain.astype(F32)[:, None]
    wide = packed_wide(gain2, expand_gate, expand_value, contract_weight.T, count, lanes)
    wide = all_to_all(after(wide, *first)).reshape(width, 3 * lanes)

    yv = jnp.concatenate([dot(piece, weight_yv, ((1,), (0,))) for piece in first])
    token_f32, token_bf16 = ((total, LANES), F32), ((total, LANES), BF16)
    padded = ((total + 8, LANES), F32)
    y, vp, c, cb = on_chip(
        functools.partial(filter_kernel, th=th, taps=taps),
        slot,
        [yv, tap_rows],
        [token_f32, padded, token_f32, token_bf16],
    )
    cb_other = core_swap(cb)
    gate_near, gate_far = own_half(gates), far_half(gates)
    gi, ga, hp, ob = on_chip(
        functools.partial(state_kernel, th=th),
        slot,
        [cb, cb_other, gate_near, gate_far, c, y, gate_rows_of],
        [token_f32, token_f32, padded, token_bf16],
        [token_f32, token_f32],
    )
    out_both = jnp.concatenate([weight_out, weights_other[:, 2 * LANES :]], axis=1)
    weight_ge, weight_c = wide[:, : 2 * lanes], wide[:, 2 * lanes :]
    dz = dot(given_out, weight_c, ((1,), (0,)))
    merged = grouped(after(ob, wide))
    merged[0] = after(merged[0], dz)
    r = x + scattered((merged, out_both))[0]

    s2 = lax.rsqrt(jnp.mean(r * r, axis=-1, keepdims=True) + EPSILON)
    second = gathered((r * s2).astype(BF16))
    second = jnp.concatenate(second)
    zb, dge = on_chip(
        functools.partial(feed_kernel, th=th),
        slot,
        [dot(second, weight_ge, ((1,), (0,))), dz],
        [((total, lanes), BF16), ((total, 2 * lanes), BF16)],
    )
    ge_both = jnp.concatenate([weight_ge, core_swap(weight_ge)], axis=1)
    c_both = jnp.concatenate([weight_c, core_swap(weight_c)], axis=1)
    (back2,) = scattered((grouped(dge), ge_both))
    dr = (
        cotangent.astype(F32)
        + s2 * back2
        - r * (s2 * s2 * s2) * jnp.mean(back2 * r, axis=-1, keepdims=True)
    )
    dq = gathered(dr.astype(BF16))

    wide_grad = jnp.concatenate(
        lax.optimization_barrier(
            (
                dot(second, dge, ((0,), (0,))).astype(BF16),
                dot(given_out, zb, ((0,), (0,))).astype(BF16),
            )
        ),
        axis=1,
    )
    *dq, wide_grad = lax.optimization_barrier((*dq, wide_grad))
    (out_sum,) = scattered((grouped(after(zb, back2)), c_both))
    out_half = (r + out_sum).astype(BF16)
    wide_grad = all_to_all(wide_grad.reshape(count, part, 3 * lanes))
    gate_grad_out, value_grad_out, contract_grad_out, gain2_part = unpacked_wide(
        wide_grad, gain2, expand_gate, expand_value, lanes
    )

    dob = jnp.concatenate([dot(piece, weight_out, ((1,), (0,))) for piece in dq])
    dy, dpp, dc, sums = on_chip(
        functools.partial(adjoint_kernel, th=th),
        slot,
        [dob, y, hp, gi, ga, c, gate_rows_of],
        [token_bf16, ((total, 2 * LANES), BF16), token_f32, ((8, LANES), F32)],
        [token_f32, token_f32, token_f32],
    )
    dpp_other = core_swap(dpp)
    dv, tap_sums = on_chip(
        functools.partial(unfilter_kernel, th=th, taps=taps),
        slot,
        [dpp, dpp_other, gate_near, own_half(gates_other), dc, vp, tap_rows],
        [token_bf16, ((8, LANES), F32)],
        [padded],
    )
    dyv = jnp.concatenate([dy, dv], axis=1)
    weight_grad = jnp.concatenate(
        lax.optimization_barrier(
            (
                dot(jnp.concatenate(first), dyv, ((0,), (0,))).astype(BF16),
                dot(jnp.concatenate(dq), ob, ((0,), (0,))).astype(BF16),
            )
        ),
        axis=1,
    )
    weight_grad = weight_grad.reshape(count, part, 3 * LANES)
    own_grad, far_grad = dot(cb, dpp, ((0,), (0,))), dot(cb_other, dpp, ((0,), (0,)))
    gate_grad = jnp.concatenate(
        [jnp.where(core == 0, own_grad, far_grad), jnp.where(core == 0, far_grad, own_grad)], axis=0
    )
    gate_grad = jnp.pad(
        gate_grad.reshape(count, gate_rows, 2 * LANES), ((0, 0), (0, extra - gate_rows), (0, 0))
    )
    small_grad = jnp.concatenate(
        [tap_sums[:taps], sums[:2], sums[2:3] * jax.nn.sigmoid(param_row)], axis=0
    )
    small_grad = jnp.concatenate(
        [
            jnp.where(core == 0, small_grad, 0.0),
            jnp.where(core == 0, 0.0, small_grad),
        ],
        axis=1,
    )
    small_grad = small_grad.reshape(taps + 3, count, gate_rows).transpose(1, 0, 2)
    small_grad = jnp.pad(
        small_grad, ((0, 0), (0, extra - taps - 3), (0, LANES - gate_rows))
    )
    gate_grad = jnp.concatenate([gate_grad, small_grad], axis=-1).astype(BF16)
    weight_grad = all_to_all(after(jnp.concatenate([gate_grad, weight_grad], axis=1), wide_grad))
    low = jnp.stack([weight_grad[c] for c in chip_of[:local_blocks]])
    high = jnp.stack([weight_grad[c] for c in chip_of[local_blocks:]])
    kept = jnp.where(core == 0, low, high)
    given = core_swap(jnp.where(core == 0, high, low))
    halves = jnp.stack([jnp.where(core == 0, kept, given), jnp.where(core == 0, given, kept)])
    (
        gelu_grad_out,
        scan_grad_out,
        output_grad_out,
        input_gate_out,
        decay_gate_out,
        gain1_part,
    ) = unpacked_narrow(halves, gain1, gelu_weight, scan_weight, gate_rows)
    small_sum = halves[:, :, : taps + 3, 2 * LANES : 2 * LANES + gate_rows].astype(F32)
    small_sum = (small_sum[0] + small_sum[1]).transpose(1, 0, 2)

    yv_both = jnp.concatenate([weight_yv, weights_other[:, : 2 * LANES]], axis=1)
    back1 = grouped(after(dyv, wide_grad))
    back1[0] = after(back1[0], gain1_part, gain2_part, out_half)
    (back1,) = scattered((back1, yv_both))
    in_half = dr + s1 * back1 - x * (s1 * s1 * s1) * jnp.mean(back1 * x, axis=-1, keepdims=True)

    gain_parts = jnp.stack([jnp.sum(gain1_part, axis=1), jnp.sum(gain2_part, axis=1)])
    gain_grads = gain_parts + core_swap(gain_parts)

    def both_halves(half):
        swapped = core_swap(half)
        return jnp.concatenate(
            [jnp.where(core == 0, half, swapped), jnp.where(core == 0, swapped, half)], axis=0
        )

    return (
        both_halves(out_half),
        both_halves(in_half),
        gain_grads[0],
        gelu_grad_out,
        scan_grad_out,
        small_sum[:taps],
        input_gate_out,
        small_sum[taps],
        decay_gate_out,
        small_sum[taps + 1],
        small_sum[taps + 2],
        output_grad_out.T,
        gain_grads[1],
        gate_grad_out,
        value_grad_out,
        contract_grad_out.T,
    )


def solution(mesh):
    in_specs = (
        P("seq", None),
        P("seq"),
        P("seq", "head"),
        P("seq", "head"),
        P(None, "head", "seq"),
        P("head", "seq", None),
        P("head", "seq"),
        P("head", "seq", None),
        P("head", "seq"),
        P("head", "seq"),
        P("head", "seq"),
        P("seq"),
        P("seq", "head"),
        P("seq", "head"),
        P("head", "seq"),
        P("seq", None),
    )
    out_specs = (
        P("seq", None),
        P("seq", None),
        P("seq"),
        P("seq", "head"),
        P("seq", "head"),
        P(None, "head", "seq"),
        P("head", "seq", None),
        P("head", "seq"),
        P("head", "seq", None),
        P("head", "seq"),
        P("head", "seq"),
        P("head", "seq"),
        P("seq"),
        P("seq", "head"),
        P("seq", "head"),
        P("head", "seq"),
    )
    return jax.shard_map(shards, mesh=mesh, in_specs=in_specs, out_specs=out_specs, check_vma=False)
```

```python
import functools

import jax
import jax.numpy as jnp
from jax import lax
from jax.experimental import pallas as pl
from jax.experimental.pallas import tpu as pltpu
from jax.sharding import PartitionSpec as P

BF16 = jnp.bfloat16
F32 = jnp.float32
EPSILON = 1e-06
BOTH = ("seq", "head")
LANES = 128
CHUNK = 128
GELU_A = 0.7978845608028654
GELU_B = 0.044715
VMEM_BYTES = 56 * 1024 * 1024


def xor_send(value, mask_first, mask_second=None, allowed=None):
    count = lax.axis_size("seq")
    masks = (mask_first, mask_first if mask_second is None else mask_second)
    pairs = [
        (chip * 2 + core, (chip ^ masks[core]) * 2 + core)
        for chip in range(count)
        for core in range(2)
        if allowed is None or allowed(chip, chip ^ masks[core])
    ]
    return lax.ppermute(value, BOTH, pairs)


def core_swap(value):
    return lax.ppermute(value, "head", [(0, 1), (1, 0)])


def row_send(value, to):
    pairs = [
        (row * 8 + device, to[row] * 8 + device) for row in sorted(to) for device in range(8)
    ]
    return lax.ppermute(value, BOTH, pairs)


PAIRED = {0: 1, 1: 0, 2: 3, 3: 2}
CROSSED = {1: 2, 2: 1}
OUTWARD = {1: 0, 2: 3}


def row_gathered(rows):
    count = lax.axis_size("seq")
    if count != 16:
        return [rows] + [xor_send(rows, 4 * g) for g in range(1, count // 4)]
    one = row_send(rows, PAIRED)
    cross = row_send(rows, CROSSED)
    far = row_send(one, CROSSED)
    return [rows, one, far + row_send(cross, OUTWARD), cross + row_send(far, OUTWARD)]


def gathered(rows, early=()):
    own = []
    columns = row_gathered(rows)
    for g, block in enumerate(columns):
        pair = jnp.concatenate([block, xor_send(block, 2, 1)], axis=0)
        if g == len(columns) - 1 and early:
            pair = after(pair, *early)
        own.append(jnp.concatenate([pair, xor_send(pair, 1, 2)], axis=0))
    return own + [core_swap(group) for group in own]


def scattered(*products):
    count = lax.axis_size("seq") // 4
    rows = products[0][0][0].shape[0] // 4
    parts = len(products)

    def sent(arrays, *masks):
        moved = xor_send(jnp.concatenate([a.astype(BF16) for a in arrays]), *masks)
        return [a.astype(F32) for a in jnp.split(moved, parts)]

    own = None
    arriving = []
    for g in list(range(1, count)) + [0]:
        sums = [dot(groups[g], right, ((1,), (1,))).astype(BF16) for groups, right in products]
        more = sent([a[2 * rows :] for a in sums], 1, 2)
        sums = [a[: 2 * rows].astype(F32) + b for a, b in zip(sums, more)]
        more = sent([a[rows:] for a in sums], 2, 1)
        sums = [a[:rows] + b for a, b in zip(sums, more)]
        if g:
            arriving.append(sent(sums, 4 * g))
        else:
            own = sums
    for more in arriving:
        own = [a + b for a, b in zip(own, more)]
    return own


INWARD = {0: 1, 3: 2}


def row_scattered(parts):
    own = parts[0].astype(F32)
    if len(parts) != 4:
        moved = [xor_send(part, 4 * g).astype(F32) for g, part in enumerate(parts) if g]
        return functools.reduce(jnp.add, moved, own)
    _, one, two, three = parts
    two, three = (
        two.astype(F32) + row_send(three, INWARD).astype(F32),
        three.astype(F32) + row_send(two, INWARD).astype(F32),
    )
    own = own + row_send(three.astype(BF16), CROSSED).astype(F32)
    one = one.astype(F32) + row_send(two.astype(BF16), CROSSED).astype(F32)
    return own + row_send(one.astype(BF16), PAIRED).astype(F32)


def near_gathered(rows):
    pair = jnp.concatenate([rows, xor_send(rows, 2, 1)], axis=0)
    own = jnp.concatenate([pair, xor_send(pair, 1, 2)], axis=0)
    return jnp.concatenate([own, core_swap(own)], axis=0)


def near_scattered(rows, *right):
    half = rows.shape[0] // 2
    th = half // 4
    both = (rows[:half], core_swap(rows[half:]))
    if len(right) == 1:
        both = (jnp.concatenate(both, axis=1),)
    partial = sum(dot(a, b, ((1,), (1,))) for a, b in zip(both, right)).astype(BF16)
    pair = partial[: 2 * th].astype(F32) + xor_send(partial[2 * th :], 1, 2).astype(F32)
    return pair[:th] + xor_send(pair[th:].astype(BF16), 2, 1).astype(F32)


def near_exchanged(pieces):
    count = lax.axis_size("seq")
    fours = [list(range(first, first + 4)) for first in range(0, count, 4)]
    return lax.all_to_all(pieces, "seq", 0, 0, tiled=True, axis_index_groups=fours)


def next_four(value, step):
    count = lax.axis_size("seq")
    pairs = [
        (chip * 2 + core, (chip + 4 * step) * 2 + core)
        for chip in range(count)
        for core in range(2)
        if 0 <= chip + 4 * step < count
    ]
    return lax.ppermute(value, BOTH, pairs)


def carried(pair, place, reverse):
    count = lax.axis_size("seq") // 4
    pairs = jnp.stack([pair] + [xor_send(pair, 4 * g) for g in range(1, count)])
    state = jnp.zeros_like(pair[:1])
    for lap in range(count - 1):
        source = count - 1 - lap if reverse else lap
        one = lax.dynamic_index_in_dim(pairs, place ^ source, 0, False)
        ahead = source > place if reverse else source < place
        state = jnp.where(ahead, one[0:1] * state + one[1:2], state)
    return state


def grouped(rows):
    half = rows.shape[0] // 2
    both = jnp.concatenate([rows[:half], core_swap(rows[half:])], axis=1)
    return list(both.reshape(lax.axis_size("seq") // 4, -1, both.shape[1]))


def after(value, *others):
    return lax.optimization_barrier((value,) + others)[0]


def all_to_all(pieces):
    return lax.all_to_all(pieces, "seq", 0, 0, tiled=True)


def params(**more):
    return pltpu.CompilerParams(vmem_limit_bytes=VMEM_BYTES, **more)


def pack_wide(gain, gate, value, contract, out, *, chips):
    lanes = gate.shape[1]
    live = pl.program_id(0) < chips
    scale = jnp.where(live, gain[...], 0.0)
    out[0, :, :lanes] = (gate[...].astype(F32) * scale).astype(BF16)
    out[0, :, lanes : 2 * lanes] = (value[...].astype(F32) * scale).astype(BF16)
    out[0, :, 2 * lanes :] = jnp.where(live, contract[...].astype(F32), 0.0).astype(BF16)


def packed_wide(gain, gate, value, contract, count, lanes):
    part, hidden = gate.shape
    chips = hidden // lanes
    column = pl.BlockSpec((part, lanes), lambda j: (0, jnp.minimum(j, chips - 1)))
    return pl.pallas_call(
        functools.partial(pack_wide, chips=chips),
        out_shape=jax.ShapeDtypeStruct((count, part, 3 * lanes), BF16),
        grid=(count,),
        in_specs=[
            pl.BlockSpec((part, 1), lambda j: (0, 0)),
            column,
            column,
            column,
        ],
        out_specs=pl.BlockSpec((1, part, 3 * lanes), lambda j: (j, 0, 0)),
        compiler_params=params(),
    )(gain, gate, value, contract)


def unpack_wide(grads, gain, gate, value, gate_out, value_out, contract_out, sums):
    lanes = gate.shape[1] // grads.shape[0]

    @pl.when(pl.program_id(0) == 0)
    def _():
        sums[...] = jnp.zeros_like(sums)

    total = sums[...]
    for i in range(grads.shape[0]):
        at = slice(i * lanes, (i + 1) * lanes)
        gate_hat = grads[i, :, :lanes].astype(F32)
        value_hat = grads[i, :, lanes : 2 * lanes].astype(F32)
        gate_out[:, at] = gate_hat * gain[...]
        value_out[:, at] = value_hat * gain[...]
        contract_out[:, at] = grads[i, :, 2 * lanes :].astype(F32)
        both = gate_hat * gate[:, at].astype(F32) + value_hat * value[:, at].astype(F32)
        for start in range(0, lanes, LANES):
            total = total + both[:, start : start + LANES]
    sums[...] = total


def unpacked_wide(grads, gain, gate, value, lanes):
    part, hidden = gate.shape
    chips = hidden // lanes
    at_once = 3 if chips % 3 == 0 else 1
    column = pl.BlockSpec((part, at_once * lanes), lambda j: (0, j))
    return pl.pallas_call(
        unpack_wide,
        out_shape=[
            jax.ShapeDtypeStruct((part, hidden), F32),
            jax.ShapeDtypeStruct((part, hidden), F32),
            jax.ShapeDtypeStruct((part, hidden), F32),
            jax.ShapeDtypeStruct((part, LANES), F32),
        ],
        grid=(chips // at_once,),
        in_specs=[
            pl.BlockSpec((at_once, part, 3 * lanes), lambda j: (j, 0, 0)),
            pl.BlockSpec((part, 1), lambda j: (0, 0)),
            column,
            column,
        ],
        out_specs=[
            column,
            column,
            column,
            pl.BlockSpec((part, LANES), lambda j: (0, 0)),
        ],
        compiler_params=params(),
    )(grads, gain, gate, value)


HALVES = (((0, 1, 2), (4, 5, 3)), ((6, 7, None), (8, 9, None)))


def pack_narrow(gain, gelu, scan, output, in_gate, de_gate, small, yv_out, wo_out, *, extra):
    for core in range(2):
        for side in range(2):
            halves = HALVES[side][core]
            few = yv_out.at[core, side, extra : 2 * extra, :]
            few[...] = jnp.zeros_like(few)
            for place, half in enumerate(halves):
                at = slice(place * LANES, (place + 1) * LANES)
                more = slice((3 + place) * LANES, (4 + place) * LANES)
                if half is None:
                    yv_out[core, side, :, at] = jnp.zeros_like(yv_out[core, side, :, at])
                    yv_out[core, side, :, more] = jnp.zeros_like(yv_out[core, side, :, more])
                    wo_out[core, side, :, at] = jnp.zeros_like(wo_out[core, side, :, at])
                    continue
                block, odd = half // 2, half % 2
                column = slice(half * LANES, (half + 1) * LANES)
                lanes = slice(odd * LANES, (odd + 1) * LANES)
                yv_out[core, side, :extra, at] = in_gate[block, :, lanes]
                yv_out[core, side, :extra, more] = de_gate[block, :, lanes]
                if place != 1:
                    spot = slice((place // 2) * LANES, (place // 2 + 1) * LANES)
                    yv_out[core, side, extra : 2 * extra, spot] = small[block]
                yv_out[core, side, 2 * extra :, at] = (
                    gelu[:, column].astype(F32) * gain[...]
                ).astype(BF16)
                yv_out[core, side, 2 * extra :, more] = (
                    scan[:, column].astype(F32) * gain[...]
                ).astype(BF16)
                wo_out[core, side, :, at] = output[:, column]


def packed_narrow(gain, gelu, scan, output, in_gate, de_gate, small):
    part = gelu.shape[0]
    extra = small.shape[1]
    return in_vmem(
        functools.partial(pack_narrow, extra=extra),
        [gain, gelu, scan, output, in_gate, de_gate, small],
        [((2, 2, 2 * extra + part, 6 * LANES), BF16), ((2, 2, part, 3 * LANES), BF16)],
    )


def unpack_narrow(
    yv, wo, gain, gelu, scan, gelu_out, scan_out, output_out, in_out, de_out, sums, *, extra
):
    rows = in_out.shape[1]
    sums[...] = jnp.zeros_like(sums)
    for core in range(2):
        for side in range(2):
            for place, half in enumerate(HALVES[side][core]):
                if half is None:
                    continue
                block, odd = half // 2, half % 2
                at = slice(place * LANES, (place + 1) * LANES)
                more = slice((3 + place) * LANES, (4 + place) * LANES)
                column = slice(half * LANES, (half + 1) * LANES)
                lanes = slice(odd * LANES, (odd + 1) * LANES)
                gelu_hat = yv[core, side, 2 * extra :, at].astype(F32)
                scan_hat = yv[core, side, 2 * extra :, more].astype(F32)
                gelu_out[:, column] = gelu_hat * gain[...]
                scan_out[:, column] = scan_hat * gain[...]
                output_out[:, column] = wo[core, side, :, at].astype(F32)
                in_out[block, :, lanes] = yv[core, side, :extra, at].astype(F32)[:rows]
                de_out[block, :, lanes] = yv[core, side, :extra, more].astype(F32)[:rows]
                sums[...] += gelu_hat * gelu[:, column].astype(F32) + scan_hat * scan[
                    :, column
                ].astype(F32)


def unpacked_narrow(yv, wo, gain, gelu, scan, local_blocks, gate_rows, extra):
    part, width = gelu.shape
    gate = ((local_blocks, gate_rows, 2 * LANES), F32)
    return in_vmem(
        functools.partial(unpack_narrow, extra=extra),
        [yv, wo, gain, gelu, scan],
        [((part, width), F32)] * 3 + [gate, gate, ((part, LANES), F32)],
    )


def gelu_parts(w):
    inner = jnp.tanh(GELU_A * (w + GELU_B * w * w * w))
    return 0.5 * w * (1.0 + inner), inner


def gelu_slope(w, inner):
    return 0.5 * (1.0 + inner) + 0.5 * w * (1.0 - inner * inner) * GELU_A * (
        1.0 + 3.0 * GELU_B * w * w
    )


def rate_parts(ga, soft_row):
    log_rate = -8.0 * ga * soft_row
    twice = 2.0 * log_rate
    near = -twice * (
        1.0 + twice * (0.5 + twice * (1.0 / 6 + twice * (1.0 / 24 + twice * (1.0 / 120))))
    )
    rate = jnp.exp(log_rate)
    far = 1.0 - jnp.exp(twice)
    return rate, jnp.sqrt(jnp.where(twice > -0.1, near, far))


def filter_kernel(slot, yv, before, rows, y, vp, c, cb, *, th, taps):
    total, wide = y.shape
    vp[0:8, :] = before[...]

    def order(b, carry):
        block = yv[pl.ds(pl.multiple_of(slot[b] * th, th), th), :]
        y[pl.ds(pl.multiple_of(b * th, th), th), :] = block[:, :wide]
        vp[pl.ds(pl.multiple_of(b * th + 8, 8), th), :] = block[:, wide:]
        return carry

    lax.fori_loop(0, total // th, order, 0)

    def chunk(i, carry):
        start = pl.multiple_of(i * CHUNK, CHUNK)
        window = vp[pl.ds(start, CHUNK + 8), :]
        out = rows[0:1, :] * window[8 : 8 + CHUNK]
        for k in range(1, taps):
            out = out + rows[k : k + 1, :] * window[8 - k : 8 - k + CHUNK]
        c[pl.ds(start, CHUNK), :] = out
        cb[pl.ds(start, CHUNK), :] = out.astype(BF16)
        return carry

    lax.fori_loop(0, total // CHUNK, chunk, 0)


def put(ref, at, value):
    for i in range(ref.shape[0]):
        ref[i, at, :] = value[:, i * LANES : (i + 1) * LANES]


def got(ref, at):
    return jnp.concatenate([ref[i, at, :] for i in range(ref.shape[0])], axis=1)


def states_kernel(cb, far, whole, near_gates, far_gates, c, rows, gi, ga, hp, p, ends, pair, a):
    total, wide = c.shape
    length = total // 8
    bias_i, bias_a, soft = rows[0:1, :], rows[1:2, :], rows[2:3, :]

    def chunk(i, carry):
        at = pl.ds(pl.multiple_of(i * CHUNK, CHUNK), CHUNK)
        full = jnp.dot(cb[at, : 2 * LANES], whole[...], preferred_element_type=F32)
        half = jnp.dot(cb[at, 2 * LANES :], near_gates[...], preferred_element_type=F32)
        half = half + jnp.dot(far[at, :], far_gates[...], preferred_element_type=F32)
        pre_i = jnp.concatenate([full[:, : 2 * LANES], half[:, :LANES]], axis=1)
        pre_a = jnp.concatenate([full[:, 2 * LANES :], half[:, LANES:]], axis=1)
        open_i = jax.nn.sigmoid(pre_i + bias_i)
        open_a = jax.nn.sigmoid(pre_a + bias_a)
        rate, scale = rate_parts(open_a, soft)
        gi[at, :] = open_i
        ga[at, :] = open_a
        put(a, at, rate)
        put(hp, at, scale * open_i * c[at, :])
        return carry

    lax.fori_loop(0, total // CHUNK, chunk, 0)

    tiles = wide // LANES

    def step(t, carry):
        at = pl.ds(t, 8, stride=length)
        out = []
        for i, (h, q) in enumerate(carry):
            rate = a[i, at, :]
            h = rate * h + hp[i, at, :]
            q = q * rate
            hp[i, at, :] = h
            p[i, at, :] = q
            out.append((h, q))
        return tuple(out)

    start = ((jnp.zeros((8, LANES), F32), jnp.ones((8, LANES), F32)),) * tiles
    last, product = (
        jnp.concatenate(parts, axis=1)
        for parts in zip(*lax.fori_loop(0, length, step, start, unroll=8))
    )
    ends[0:8, :] = product
    ends[8:16, :] = last
    rates, state = product[0:1], last[0:1]
    for j in range(1, 8):
        state = product[j : j + 1] * state + last[j : j + 1]
        rates = rates * product[j : j + 1]
    pair[...] = jnp.zeros_like(pair)
    pair[0:1, :] = rates
    pair[1:2, :] = state


def merge_kernel(slot, hp, p, ends, carry_in, y, h, ob, *, th):
    total = y.shape[0]
    per = total // 8 // th
    enter = carry_in[...]
    h[0:8, :] = jnp.broadcast_to(enter, (8, enter.shape[1]))
    for j in range(8):

        def finish(i, carry, j=j, enter=enter):
            b = j * per + i
            at = pl.ds(pl.multiple_of(b * th, th), th)
            state = got(hp, at) + got(p, at) * enter
            h[pl.ds(pl.multiple_of(b * th + 8, 8), th), :] = state
            out, _ = gelu_parts(y[at, :])
            ob[pl.ds(pl.multiple_of(slot[b] * th, th), th), :] = (state * out).astype(BF16)
            return carry

        lax.fori_loop(0, per, finish, 0)
        enter = ends[8 + j : 9 + j, :] + ends[j : j + 1, :] * enter


def adjoint_kernel(slot, dob, y, h, ga, rows, dy, lam, q, ends, pair, a, *, th):
    total, wide = y.shape
    length = total // 8
    soft = rows[2:3, :]

    def order(b, carry):
        at = pl.ds(pl.multiple_of(b * th, th), th)
        there = pl.ds(pl.multiple_of(slot[b] * th, th), th)
        block = dob[there, :]
        w = y[at, :]
        out, inner = gelu_parts(w)
        put(lam, at, block * out)
        state = h[pl.ds(pl.multiple_of(b * th + 8, 8), th), :]
        dy[there, :] = (block * state * gelu_slope(w, inner)).astype(BF16)
        put(a, at, jnp.exp(-8.0 * ga[at, :] * soft))
        return carry

    lax.fori_loop(0, total // th, order, 0)

    tiles = wide // LANES

    def step(t, carry):
        at = pl.ds(length - 1 - t, 8, stride=length)
        out = []
        for i, (later, product) in enumerate(carry):
            here = lam[i, at, :] + later
            lam[i, at, :] = here
            q[i, at, :] = product
            rate = a[i, at, :]
            out.append((rate * here, product * rate))
        return tuple(out)

    start = ((jnp.zeros((8, LANES), F32), jnp.ones((8, LANES), F32)),) * tiles
    first, product = (
        jnp.concatenate(parts, axis=1)
        for parts in zip(*lax.fori_loop(0, length, step, start, unroll=8))
    )
    ends[0:8, :] = product
    ends[8:16, :] = first
    rates, state = product[7:8], first[7:8]
    for j in range(6, -1, -1):
        state = product[j : j + 1] * state + first[j : j + 1]
        rates = rates * product[j : j + 1]
    pair[...] = jnp.zeros_like(pair)
    pair[0:1, :] = rates
    pair[1:2, :] = state


def gates_kernel(lam, q, ends, carry_in, h, gi, ga, c, rows, dpi, dpa, dc, sums):
    total, wide = c.shape
    length = total // 8
    soft = rows[2:3, :]
    step = min(length, 64)
    enter = carry_in[...]
    carry = (jnp.zeros((1, wide), F32),) * 3
    for j in range(7, -1, -1):

        def finish(i, carry, j=j, enter=enter):
            start = pl.multiple_of(j * length + i * step, 8)
            at = pl.ds(start, step)
            state_grad = got(lam, at) + got(q, at) * enter
            before = h[pl.ds(start, step + 8), :][7 : 7 + step]
            open_i, open_a, filtered = gi[at, :], ga[at, :], c[at, :]
            rate, scale = rate_parts(open_a, soft)
            dla = state_grad * before * rate - state_grad * open_i * filtered * rate * rate / scale
            grad_i = state_grad * scale * filtered * open_i * (1.0 - open_i)
            slope = -8.0 * open_a * dla
            grad_a = soft * slope * (1.0 - open_a)
            dpi[at, :] = grad_i.astype(BF16)
            dpa[at, :] = grad_a.astype(BF16)
            dc[at, :] = state_grad * scale * open_i
            return (
                carry[0] + jnp.sum(grad_i, axis=0, keepdims=True),
                carry[1] + jnp.sum(grad_a, axis=0, keepdims=True),
                carry[2] + jnp.sum(slope, axis=0, keepdims=True),
            )

        carry = lax.fori_loop(0, length // step, finish, carry)
        enter = ends[8 + j : 9 + j, :] + ends[j : j + 1, :] * enter
    sums[...] = jnp.zeros_like(sums)
    for row in range(3):
        sums[row : row + 1, :] = carry[row]


def ungate_kernel(dpi, dpa, far, in_whole, de_whole, near_gates, far_gates, dc, vp, dcp, sums, *, taps):
    total = dc.shape[0]
    last = (((1,), (1,)), ((), ()))
    full, half = slice(0, 2 * LANES), slice(2 * LANES, 3 * LANES)
    turned = lambda left, right: lax.dot_general(left, right, last, preferred_element_type=F32)

    def chunk(i, carry):
        start = pl.multiple_of(i * CHUNK, CHUNK)
        at = pl.ds(start, CHUNK)
        whole = turned(dpi[at, full], in_whole[...]) + turned(dpa[at, full], de_whole[...])
        middle = (
            turned(dpi[at, half], near_gates[:, :LANES])
            + turned(dpa[at, half], near_gates[:, LANES:])
            + turned(far[at, :], far_gates[...])
        )
        out = dc[at, :] + jnp.concatenate([whole, middle], axis=1)
        dcp[at, :] = out
        window = vp[pl.ds(start, CHUNK + 8), :]
        return tuple(
            carry[k] + jnp.sum(out * window[8 - k : 8 - k + CHUNK], axis=0, keepdims=True)
            for k in range(taps)
        )

    zero = jnp.zeros((1, dc.shape[1]), F32)
    carry = lax.fori_loop(0, total // CHUNK, chunk, (zero,) * taps)
    sums[...] = jnp.zeros_like(sums)
    for k in range(taps):
        sums[k : k + 1, :] = carry[k]


def unfilter_kernel(slot, dc, following, rows, dv, dcp, *, th, taps):
    total = dc.shape[0]
    dcp[0:total, :] = dc[...]
    dcp[total : total + 8, :] = following[...]

    def order(b, carry):
        window = dcp[pl.ds(pl.multiple_of(b * th, th), th + 8), :]
        out = rows[0:1, :] * window[0:th]
        for k in range(1, taps):
            out = out + rows[k : k + 1, :] * window[k : k + th]
        dv[pl.ds(pl.multiple_of(slot[b] * th, th), th), :] = out.astype(BF16)
        return carry

    lax.fori_loop(0, total // th, order, 0)


def feed_kernel(ge, dz, zb, dge, *, th):
    lanes = dz.shape[1]

    def block(b, carry):
        at = pl.ds(pl.multiple_of(b * th, th), th)
        g, e, d = ge[at, :lanes], ge[at, lanes:], dz[at, :]
        act, inner = gelu_parts(g)
        zb[at, :] = (act * e).astype(BF16)
        dge[at, :lanes] = (d * e * gelu_slope(g, inner)).astype(BF16)
        dge[at, lanes:] = (d * act).astype(BF16)
        return carry

    lax.fori_loop(0, dz.shape[0] // th, block, 0)


def on_chip(kernel, slot, inputs, outs, scratch=()):
    vmem = pl.BlockSpec(memory_space=pltpu.VMEM)
    return pl.pallas_call(
        kernel,
        out_shape=[jax.ShapeDtypeStruct(shape, dtype) for shape, dtype in outs],
        in_specs=[pl.BlockSpec(memory_space=pltpu.SMEM)] + [vmem] * len(inputs),
        out_specs=[vmem] * len(outs),
        scratch_shapes=[pltpu.VMEM(shape, dtype) for shape, dtype in scratch],
        compiler_params=params(),
    )(slot, *inputs)


def in_vmem(kernel, inputs, outs, scratch=()):
    vmem = pl.BlockSpec(memory_space=pltpu.VMEM)
    return pl.pallas_call(
        kernel,
        out_shape=[jax.ShapeDtypeStruct(shape, dtype) for shape, dtype in outs],
        in_specs=[vmem] * len(inputs),
        out_specs=[vmem] * len(outs),
        scratch_shapes=[pltpu.VMEM(shape, dtype) for shape, dtype in scratch],
        compiler_params=params(),
    )(*inputs)


def dot(left, right, over):
    return lax.dot_general(left, right, (over, ((), ())), preferred_element_type=F32)


def shards(
    block_input,
    first_gain,
    gelu_weight,
    scan_weight,
    filter_taps,
    input_gate,
    input_bias,
    decay_gate,
    decay_bias,
    decay_param,
    output_weight,
    second_gain,
    expand_gate,
    expand_value,
    contract_weight,
    output_cotangent,
):
    count = lax.axis_size("seq")
    chip = lax.axis_index("seq")
    core = lax.axis_index("head")
    th = block_input.shape[0] // 2
    width = block_input.shape[1]
    part = gelu_weight.shape[0]
    taps = filter_taps.shape[0]
    local_blocks, gate_rows, block_width = input_gate.shape
    assert block_width == 2 * LANES and width == part * count and local_blocks == 5
    place = chip // 4
    fours = count // 4
    near = 8 * th
    total = 2 * count * th
    lanes_r = 3 * LANES
    slab = 4 * part

    hidden = expand_gate.shape[1]
    lanes = LANES * -(-hidden // (count * LANES))
    hidden_chips = hidden // lanes
    assert hidden_chips * lanes == hidden

    number = jnp.arange(8, dtype=jnp.int32)
    relative = (chip & 3) ^ (number // 2)
    turned = ((relative & 1) << 1) | (relative >> 1)
    slot = jnp.where(number % 2 == 0, turned, relative) + jnp.where(number % 2 == core, 0, 4)
    slot = slot.astype(jnp.int32)

    def slabs(rows):
        return jnp.concatenate(
            [lax.dynamic_slice_in_dim(rows, (place ^ j) * slab, slab, 1) for j in range(fours)],
            axis=1,
        )

    extra = max(16, gate_rows)
    more_rows = ((0, 0), (0, extra - gate_rows), (0, 0))
    gain1 = first_gain.astype(F32)[:, None]
    small = jnp.concatenate(
        [
            filter_taps.transpose(1, 0, 2),
            input_bias[:, None],
            decay_bias[:, None],
            decay_param[:, None],
        ],
        axis=1,
    )
    small = jnp.pad(
        small, ((0, 0), (0, extra - small.shape[1]), (0, LANES - small.shape[2]))
    )
    packed = packed_narrow(
        gain1,
        gelu_weight,
        scan_weight,
        output_weight.T,
        jnp.pad(input_gate, more_rows),
        jnp.pad(decay_gate, more_rows),
        small,
    )

    def both_sides(pieces):
        kept = lax.dynamic_index_in_dim(pieces, core, 0, False)
        given = core_swap(lax.dynamic_index_in_dim(pieces, 1 - core, 0, False))
        return jnp.concatenate(
            [jnp.where(core == 0, kept, given), jnp.where(core == 0, given, kept)], axis=0
        )

    packed = [near_exchanged(both_sides(piece)) for piece in packed]
    pieces_yv = row_gathered(packed[0])
    weight_yv = jnp.concatenate([piece[:, 2 * extra :].reshape(slab, -1) for piece in pieces_yv])
    heads = jnp.stack([piece[:, : 2 * extra] for piece in pieces_yv])
    heads = jnp.concatenate(
        [lax.dynamic_index_in_dim(heads, place ^ j, 0, False) for j in range(fours)]
    )
    gates = heads[:, :gate_rows].reshape(block_width, 2 * lanes_r)
    small = heads[:, extra : extra + taps + 3]
    small = [
        small[:, :, i * LANES : i * LANES + gate_rows].transpose(1, 0, 2).reshape(taps + 3, -1)
        for i in range(2)
    ]
    own_half = lambda a, axis=0: lax.dynamic_slice_in_dim(a, core * LANES, LANES, axis)
    far_half = lambda a, axis=0: lax.dynamic_slice_in_dim(a, (1 - core) * LANES, LANES, axis)
    small = jnp.concatenate([small[0], own_half(small[1], 1)], axis=1).astype(F32)
    tap_rows = jnp.pad(small[:taps], ((0, 8 - taps), (0, 0)))
    param_row = small[taps + 2 :]
    gate_rows_of = jnp.pad(
        jnp.concatenate([small[taps : taps + 2], jax.nn.softplus(param_row)], axis=0),
        ((0, 5), (0, 0)),
    )
    in_whole, de_whole = gates[:, : 2 * LANES], gates[:, lanes_r : lanes_r + 2 * LANES]
    half_gates = jnp.concatenate([gates[:, 2 * LANES : lanes_r], gates[:, lanes_r + 2 * LANES :]], 1)

    x = lax.dynamic_slice_in_dim(block_input, core * th, th, 0).astype(F32)
    s1 = lax.rsqrt(jnp.mean(x * x, axis=-1, keepdims=True) + EPSILON)
    first = near_gathered(slabs((x * s1).astype(BF16)))
    cotangent = lax.dynamic_slice_in_dim(output_cotangent, core * th, th, 0)
    given_out = jnp.concatenate(gathered(after(cotangent, first)))
    pieces_out = row_gathered(after(packed[1], *pieces_yv))
    weight_out = jnp.concatenate([piece.reshape(slab, lanes_r) for piece in pieces_out])

    gain2 = second_gain.astype(F32)[:, None]
    wide = packed_wide(gain2, expand_gate, expand_value, contract_weight.T, count, lanes)
    wide = all_to_all(after(wide, weight_yv)).reshape(width, 3 * lanes)

    yv = dot(first, weight_yv, ((1,), (0,)))
    tail = lax.dynamic_slice_in_dim(yv[:, lanes_r:], slot[7] * th + th - 8, 8, 0)
    token_f32, token_bf16 = ((near, lanes_r), F32), ((near, lanes_r), BF16)
    padded = ((near + 8, lanes_r), F32)
    few = ((8, lanes_r), F32)
    tiled = ((3, near, LANES), F32)
    y, vp, c, cb = on_chip(
        functools.partial(filter_kernel, th=th, taps=taps),
        slot,
        [yv, next_four(tail, 1), tap_rows],
        [token_f32, padded, token_f32, token_bf16],
    )
    cb_far = core_swap(cb[:, 2 * LANES :])
    near_gates, far_gates = own_half(half_gates), far_half(half_gates)
    gi, ga, hp, p, ends, pair = in_vmem(
        states_kernel,
        [
            cb,
            cb_far,
            jnp.concatenate([in_whole, de_whole], axis=1),
            near_gates,
            far_gates,
            c,
            gate_rows_of,
        ],
        [token_f32, token_f32, tiled, tiled, ((16, lanes_r), F32), few],
        [tiled],
    )
    h, ob = on_chip(
        functools.partial(merge_kernel, th=th),
        slot,
        [hp, p, ends, carried(pair, place, False), y],
        [padded, token_bf16],
    )
    weight_ge, weight_c = wide[:, : 2 * lanes], wide[:, 2 * lanes :]
    dz = dot(given_out, weight_c, ((1,), (0,)))
    out_both = jnp.concatenate([weight_out, core_swap(weight_out)], axis=1)
    r = x + slabs(near_scattered(ob, out_both))

    s2 = lax.rsqrt(jnp.mean(r * r, axis=-1, keepdims=True) + EPSILON)
    second = gathered((r * s2).astype(BF16), [dz])
    second = jnp.concatenate(second)
    zb, dge = in_vmem(
        functools.partial(feed_kernel, th=th),
        [dot(second, weight_ge, ((1,), (0,))), dz],
        [((total, lanes), BF16), ((total, 2 * lanes), BF16)],
    )
    ge_both = jnp.concatenate([weight_ge, core_swap(weight_ge)], axis=1)
    c_both = jnp.concatenate([weight_c, core_swap(weight_c)], axis=1)
    (back2,) = scattered((grouped(dge), ge_both))
    dr = (
        cotangent.astype(F32)
        + s2 * back2
        - r * (s2 * s2 * s2) * jnp.mean(back2 * r, axis=-1, keepdims=True)
    )
    dq = near_gathered(slabs(dr.astype(BF16)))

    wide_grad = jnp.concatenate(
        lax.optimization_barrier(
            (
                dot(second, dge, ((0,), (0,))).astype(BF16),
                dot(given_out, zb, ((0,), (0,))).astype(BF16),
            )
        ),
        axis=1,
    )
    dq, wide_grad = lax.optimization_barrier((dq, wide_grad))
    (out_sum,) = scattered((grouped(after(zb, dq)), c_both))
    out_half = (r + out_sum).astype(BF16)
    wide_grad = all_to_all(wide_grad.reshape(count, part, 3 * lanes))
    gate_grad_out, value_grad_out, contract_grad_out, gain2_part = unpacked_wide(
        wide_grad, gain2, expand_gate, expand_value, lanes
    )

    dob = dot(dq, weight_out, ((1,), (0,)))
    dy, lam, q, ends, pair = on_chip(
        functools.partial(adjoint_kernel, th=th),
        slot,
        [dob, y, h, ga, gate_rows_of],
        [token_bf16, tiled, tiled, ((16, lanes_r), F32), few],
        [tiled],
    )
    dpi, dpa, dc, sums = in_vmem(
        gates_kernel,
        [lam, q, ends, carried(pair, place, True), h, gi, ga, c, gate_rows_of],
        [token_bf16, token_bf16, token_f32, few],
    )
    half_grads = jnp.concatenate([dpi[:, 2 * LANES :], dpa[:, 2 * LANES :]], axis=1)
    dc, tap_sums = in_vmem(
        functools.partial(ungate_kernel, taps=taps),
        [
            dpi,
            dpa,
            core_swap(half_grads),
            in_whole,
            de_whole,
            near_gates,
            own_half(core_swap(half_gates)),
            dc,
            vp,
        ],
        [token_f32, few],
    )
    dv = on_chip(
        functools.partial(unfilter_kernel, th=th, taps=taps),
        slot,
        [dc, next_four(dc[:8], -1), tap_rows],
        [token_bf16],
        [padded],
    )[0]
    dyv = jnp.concatenate([dy, dv], axis=1)

    def to_owners(grad):
        grad = row_scattered(list(grad)).astype(BF16)
        grad = near_exchanged(grad)
        kept = lax.dynamic_slice_in_dim(grad, 2 * core, 2, 0)
        given = core_swap(lax.dynamic_slice_in_dim(grad, 2 * (1 - core), 2, 0))
        return jnp.stack([jnp.where(core == 0, kept, given), jnp.where(core == 0, given, kept)])

    out_grad = lax.optimization_barrier(dot(dq, ob, ((0,), (0,))).astype(BF16))
    out_grad = to_owners(out_grad.reshape(fours, 4, part, lanes_r))
    yv_grad = lax.optimization_barrier(dot(first, dyv, ((0,), (0,))).astype(BF16))
    yv_grad = yv_grad.reshape(fours, 4, part, 2 * lanes_r)

    def gate_grad(grad):
        whole = dot(cb[:, : 2 * LANES], grad[:, : 2 * LANES], ((0,), (0,)))
        own_rows = dot(cb[:, 2 * LANES :], grad[:, 2 * LANES :], ((0,), (0,)))
        far_rows = dot(cb_far, grad[:, 2 * LANES :], ((0,), (0,)))
        half = jnp.concatenate(
            [jnp.where(core == 0, own_rows, far_rows), jnp.where(core == 0, far_rows, own_rows)]
        )
        return jnp.concatenate([whole, half], axis=1)

    head_grad = jnp.concatenate([gate_grad(dpi), gate_grad(dpa)], axis=1)
    head_grad = head_grad.reshape(count, gate_rows, 2 * lanes_r)
    head_grad = jnp.pad(head_grad, ((0, 0), (0, extra - gate_rows), (0, 0)))
    small_grad = jnp.concatenate(
        [tap_sums[:taps], sums[:2], sums[2:3] * jax.nn.sigmoid(param_row)], axis=0
    )
    middle = small_grad[:, 2 * LANES :]
    nothing = jnp.zeros_like(middle)
    small_grad = [
        small_grad[:, : 2 * LANES],
        jnp.where(
            core == 0,
            jnp.concatenate([middle, nothing], axis=1),
            jnp.concatenate([nothing, middle], axis=1),
        ),
    ]
    small_grad = [
        jnp.pad(
            a.reshape(taps + 3, count, gate_rows).transpose(1, 0, 2),
            ((0, 0), (0, extra - taps - 3), (0, LANES - gate_rows)),
        )
        for a in small_grad
    ]
    small_grad = jnp.concatenate(small_grad, axis=2)
    small_grad = jnp.pad(small_grad, ((0, 0), (0, 0), (0, 2 * lanes_r - 2 * LANES)))
    head_grad = jnp.concatenate([head_grad, small_grad], axis=1).astype(BF16)
    head_grad = head_grad.reshape(fours, 4, 2 * extra, 2 * lanes_r)
    head_grad = jnp.stack(
        [lax.dynamic_index_in_dim(head_grad, place ^ j, 0, False) for j in range(fours)]
    )
    yv_grad = to_owners(jnp.concatenate([head_grad, yv_grad], axis=2))
    (
        gelu_grad_out,
        scan_grad_out,
        output_grad_out,
        input_gate_out,
        decay_gate_out,
        gain1_part,
    ) = unpacked_narrow(
        yv_grad, out_grad, gain1, gelu_weight, scan_weight, local_blocks, gate_rows, extra
    )
    small_sum = yv_grad[:, :, extra : extra + taps + 3].astype(F32)
    whole_sum = small_sum[..., :gate_rows]
    half_sum = small_sum[..., LANES : LANES + gate_rows]
    half_sum = half_sum[0] + half_sum[1]
    small_sum = jnp.stack(
        [whole_sum[0, 0], half_sum[0], whole_sum[1, 0], whole_sum[0, 1], whole_sum[1, 1]], axis=1
    )

    back1 = slabs(near_scattered(dyv, weight_yv, core_swap(weight_yv)))
    in_half = dr + s1 * back1 - x * (s1 * s1 * s1) * jnp.mean(back1 * x, axis=-1, keepdims=True)

    gain_parts = jnp.stack([jnp.sum(gain1_part, axis=1), jnp.sum(gain2_part, axis=1)])
    gain_grads = gain_parts + core_swap(gain_parts)

    def both_halves(half):
        swapped = core_swap(half)
        return jnp.concatenate(
            [jnp.where(core == 0, half, swapped), jnp.where(core == 0, swapped, half)], axis=0
        )

    return (
        both_halves(out_half),
        both_halves(in_half),
        gain_grads[0],
        gelu_grad_out,
        scan_grad_out,
        small_sum[:taps],
        input_gate_out,
        small_sum[taps],
        decay_gate_out,
        small_sum[taps + 1],
        small_sum[taps + 2],
        output_grad_out.T,
        gain_grads[1],
        gate_grad_out,
        value_grad_out,
        contract_grad_out.T,
    )


def solution(mesh):
    in_specs = (
        P("seq", None),
        P("seq"),
        P("seq", "head"),
        P("seq", "head"),
        P(None, "head", "seq"),
        P("head", "seq", None),
        P("head", "seq"),
        P("head", "seq", None),
        P("head", "seq"),
        P("head", "seq"),
        P("head", "seq"),
        P("seq"),
        P("seq", "head"),
        P("seq", "head"),
        P("head", "seq"),
        P("seq", None),
    )
    out_specs = (
        P("seq", None),
        P("seq", None),
        P("seq"),
        P("seq", "head"),
        P("seq", "head"),
        P(None, "head", "seq"),
        P("head", "seq", None),
        P("head", "seq"),
        P("head", "seq", None),
        P("head", "seq"),
        P("head", "seq"),
        P("head", "seq"),
        P("seq"),
        P("seq", "head"),
        P("seq", "head"),
        P("head", "seq"),
    )
    return jax.shard_map(shards, mesh=mesh, in_specs=in_specs, out_specs=out_specs, check_vma=False)
```

```python
import functools

import jax
import jax.numpy as jnp
from jax import lax
from jax.experimental import pallas as pl
from jax.experimental.pallas import tpu as pltpu
from jax.sharding import PartitionSpec as P

BF16 = jnp.bfloat16
F32 = jnp.float32
EPSILON = 1e-06
BOTH = ("seq", "head")
LANES = 128
CHUNK = 128
GELU_A = 0.7978845608028654
GELU_B = 0.044715
VMEM_BYTES = 56 * 1024 * 1024


def xor_send(value, mask_first, mask_second=None, allowed=None):
    count = lax.axis_size("seq")
    masks = (mask_first, mask_first if mask_second is None else mask_second)
    pairs = [
        (chip * 2 + core, (chip ^ masks[core]) * 2 + core)
        for chip in range(count)
        for core in range(2)
        if allowed is None or allowed(chip, chip ^ masks[core])
    ]
    return lax.ppermute(value, BOTH, pairs)


def core_swap(value):
    return lax.ppermute(value, "head", [(0, 1), (1, 0)])


def row_send(value, to):
    pairs = [
        (row * 8 + device, to[row] * 8 + device) for row in sorted(to) for device in range(8)
    ]
    return lax.ppermute(value, BOTH, pairs)


PAIRED = {0: 1, 1: 0, 2: 3, 3: 2}
CROSSED = {1: 2, 2: 1}
OUTWARD = {1: 0, 2: 3}


def row_gathered(rows):
    count = lax.axis_size("seq")
    if count != 16:
        return [rows] + [xor_send(rows, 4 * g) for g in range(1, count // 4)]
    one = row_send(rows, PAIRED)
    cross = row_send(rows, CROSSED)
    far = row_send(one, CROSSED)
    return [rows, one, far + row_send(cross, OUTWARD), cross + row_send(far, OUTWARD)]


def gathered(rows, early=()):
    own = []
    columns = row_gathered(rows)
    for g, block in enumerate(columns):
        pair = jnp.concatenate([block, xor_send(block, 2, 1)], axis=0)
        if g == len(columns) - 1 and early:
            pair = after(pair, *early)
        own.append(jnp.concatenate([pair, xor_send(pair, 1, 2)], axis=0))
    return own + [core_swap(group) for group in own]


def scattered(*products):
    count = lax.axis_size("seq") // 4
    rows = products[0][0][0].shape[0] // 4
    parts = len(products)

    def sent(arrays, *masks):
        moved = xor_send(jnp.concatenate([a.astype(BF16) for a in arrays]), *masks)
        return [a.astype(F32) for a in jnp.split(moved, parts)]

    own = None
    arriving = []
    for g in list(range(1, count)) + [0]:
        sums = [dot(groups[g], right, ((1,), (1,))).astype(BF16) for groups, right in products]
        more = sent([a[2 * rows :] for a in sums], 1, 2)
        sums = [a[: 2 * rows].astype(F32) + b for a, b in zip(sums, more)]
        more = sent([a[rows:] for a in sums], 2, 1)
        sums = [a[:rows] + b for a, b in zip(sums, more)]
        if g:
            arriving.append(sent(sums, 4 * g))
        else:
            own = sums
    for more in arriving:
        own = [a + b for a, b in zip(own, more)]
    return own


INWARD = {0: 1, 3: 2}


def row_scattered(parts):
    own = parts[0].astype(F32)
    if len(parts) != 4:
        moved = [xor_send(part, 4 * g).astype(F32) for g, part in enumerate(parts) if g]
        return functools.reduce(jnp.add, moved, own)
    _, one, two, three = parts
    two, three = (
        two.astype(F32) + row_send(three, INWARD).astype(F32),
        three.astype(F32) + row_send(two, INWARD).astype(F32),
    )
    own = own + row_send(three.astype(BF16), CROSSED).astype(F32)
    one = one.astype(F32) + row_send(two.astype(BF16), CROSSED).astype(F32)
    return own + row_send(one.astype(BF16), PAIRED).astype(F32)


def near_gathered(rows):
    pair = jnp.concatenate([rows, xor_send(rows, 2, 1)], axis=0)
    own = jnp.concatenate([pair, xor_send(pair, 1, 2)], axis=0)
    return jnp.concatenate([own, core_swap(own)], axis=0)


def near_scattered(rows, *right):
    half = rows.shape[0] // 2
    th = half // 4
    both = (rows[:half], core_swap(rows[half:]))
    if len(right) == 1:
        both = (jnp.concatenate(both, axis=1),)
    partial = sum(dot(a, b, ((1,), (1,))) for a, b in zip(both, right)).astype(BF16)
    pair = partial[: 2 * th].astype(F32) + xor_send(partial[2 * th :], 1, 2).astype(F32)
    return pair[:th] + xor_send(pair[th:].astype(BF16), 2, 1).astype(F32)


def near_exchanged(pieces):
    count = lax.axis_size("seq")
    fours = [list(range(first, first + 4)) for first in range(0, count, 4)]
    return lax.all_to_all(pieces, "seq", 0, 0, tiled=True, axis_index_groups=fours)


def next_four(value, step):
    count = lax.axis_size("seq")
    pairs = [
        (chip * 2 + core, (chip + 4 * step) * 2 + core)
        for chip in range(count)
        for core in range(2)
        if 0 <= chip + 4 * step < count
    ]
    return lax.ppermute(value, BOTH, pairs)


def carried(pair, place, reverse):
    count = lax.axis_size("seq") // 4
    pairs = jnp.stack([pair] + [xor_send(pair, 4 * g) for g in range(1, count)])
    state = jnp.zeros_like(pair[:1])
    for lap in range(count - 1):
        source = count - 1 - lap if reverse else lap
        one = lax.dynamic_index_in_dim(pairs, place ^ source, 0, False)
        ahead = source > place if reverse else source < place
        state = jnp.where(ahead, one[0:1] * state + one[1:2], state)
    return state


def grouped(rows):
    half = rows.shape[0] // 2
    both = jnp.concatenate([rows[:half], core_swap(rows[half:])], axis=1)
    return list(both.reshape(lax.axis_size("seq") // 4, -1, both.shape[1]))


def after(value, *others):
    return lax.optimization_barrier((value,) + others)[0]


def all_to_all(pieces):
    return lax.all_to_all(pieces, "seq", 0, 0, tiled=True)


def params(**more):
    return pltpu.CompilerParams(vmem_limit_bytes=VMEM_BYTES, **more)


def pack_wide(gain, gate, value, contract, out, *, chips):
    lanes = gate.shape[1]
    live = pl.program_id(0) < chips
    scale = jnp.where(live, gain[...], 0.0)
    out[0, :, :lanes] = (gate[...].astype(F32) * scale).astype(BF16)
    out[0, :, lanes : 2 * lanes] = (value[...].astype(F32) * scale).astype(BF16)
    out[0, :, 2 * lanes :] = jnp.where(live, contract[...].astype(F32), 0.0).astype(BF16)


def packed_wide(gain, gate, value, contract, count, lanes):
    part, hidden = gate.shape
    chips = hidden // lanes
    column = pl.BlockSpec((part, lanes), lambda j: (0, jnp.minimum(j, chips - 1)))
    return pl.pallas_call(
        functools.partial(pack_wide, chips=chips),
        out_shape=jax.ShapeDtypeStruct((count, part, 3 * lanes), BF16),
        grid=(count,),
        in_specs=[
            pl.BlockSpec((part, 1), lambda j: (0, 0)),
            column,
            column,
            column,
        ],
        out_specs=pl.BlockSpec((1, part, 3 * lanes), lambda j: (j, 0, 0)),
        compiler_params=params(),
    )(gain, gate, value, contract)


def unpack_wide(grads, turned, gain, gate, value, gate_out, value_out, contract_out, sums):
    lanes = gate.shape[1] // grads.shape[0]

    @pl.when(pl.program_id(0) == 0)
    def _():
        sums[...] = jnp.zeros_like(sums)

    total = sums[...]
    for i in range(grads.shape[0]):
        at = slice(i * lanes, (i + 1) * lanes)
        gate_hat = grads[i, :, :lanes].astype(F32)
        value_hat = grads[i, :, lanes : 2 * lanes].astype(F32)
        gate_out[:, at] = gate_hat * gain[...]
        value_out[:, at] = value_hat * gain[...]
        contract_out[:, at] = turned[i].astype(F32)
        both = gate_hat * gate[:, at].astype(F32) + value_hat * value[:, at].astype(F32)
        for start in range(0, lanes, LANES):
            total = total + both[:, start : start + LANES]
    sums[...] = total


def unpacked_wide(grads, turned, gain, gate, value, lanes):
    part, hidden = gate.shape
    chips = hidden // lanes
    at_once = 3 if chips % 3 == 0 else 1
    column = pl.BlockSpec((part, at_once * lanes), lambda j: (0, j))
    return pl.pallas_call(
        unpack_wide,
        out_shape=[
            jax.ShapeDtypeStruct((part, hidden), F32),
            jax.ShapeDtypeStruct((part, hidden), F32),
            jax.ShapeDtypeStruct((part, hidden), F32),
            jax.ShapeDtypeStruct((part, LANES), F32),
        ],
        grid=(chips // at_once,),
        in_specs=[
            pl.BlockSpec((at_once, part, 2 * lanes), lambda j: (j, 0, 0)),
            pl.BlockSpec((at_once, part, lanes), lambda j: (j, 0, 0)),
            pl.BlockSpec((part, 1), lambda j: (0, 0)),
            column,
            column,
        ],
        out_specs=[
            column,
            column,
            column,
            pl.BlockSpec((part, LANES), lambda j: (0, 0)),
        ],
        compiler_params=params(),
    )(grads, turned, gain, gate, value)


HALVES = (((0, 1, 2), (4, 5, 3)), ((6, 7, None), (8, 9, None)))


def pack_narrow(gain, gelu, scan, output, in_gate, de_gate, small, yv_out, wo_out, *, extra):
    for core in range(2):
        for side in range(2):
            halves = HALVES[side][core]
            few = yv_out.at[core, side, extra : 2 * extra, :]
            few[...] = jnp.zeros_like(few)
            for place, half in enumerate(halves):
                at = slice(place * LANES, (place + 1) * LANES)
                more = slice((3 + place) * LANES, (4 + place) * LANES)
                if half is None:
                    yv_out[core, side, :, at] = jnp.zeros_like(yv_out[core, side, :, at])
                    yv_out[core, side, :, more] = jnp.zeros_like(yv_out[core, side, :, more])
                    wo_out[core, side, :, at] = jnp.zeros_like(wo_out[core, side, :, at])
                    continue
                block, odd = half // 2, half % 2
                column = slice(half * LANES, (half + 1) * LANES)
                lanes = slice(odd * LANES, (odd + 1) * LANES)
                yv_out[core, side, :extra, at] = in_gate[block, :, lanes]
                yv_out[core, side, :extra, more] = de_gate[block, :, lanes]
                if place != 1:
                    spot = slice((place // 2) * LANES, (place // 2 + 1) * LANES)
                    yv_out[core, side, extra : 2 * extra, spot] = small[block]
                yv_out[core, side, 2 * extra :, at] = (
                    gelu[:, column].astype(F32) * gain[...]
                ).astype(BF16)
                yv_out[core, side, 2 * extra :, more] = (
                    scan[:, column].astype(F32) * gain[...]
                ).astype(BF16)
                wo_out[core, side, :, at] = output[:, column]


def packed_narrow(gain, gelu, scan, output, in_gate, de_gate, small):
    part = gelu.shape[0]
    extra = small.shape[1]
    return in_vmem(
        functools.partial(pack_narrow, extra=extra),
        [gain, gelu, scan, output, in_gate, de_gate, small],
        [((2, 2, 2 * extra + part, 6 * LANES), BF16), ((2, 2, part, 3 * LANES), BF16)],
    )


def unpack_narrow(
    yv, wo, gain, gelu, scan, gelu_out, scan_out, output_out, in_out, de_out, sums, *, extra
):
    rows = in_out.shape[1]
    sums[...] = jnp.zeros_like(sums)
    for core in range(2):
        for side in range(2):
            for place, half in enumerate(HALVES[side][core]):
                if half is None:
                    continue
                block, odd = half // 2, half % 2
                at = slice(place * LANES, (place + 1) * LANES)
                more = slice((3 + place) * LANES, (4 + place) * LANES)
                column = slice(half * LANES, (half + 1) * LANES)
                lanes = slice(odd * LANES, (odd + 1) * LANES)
                gelu_hat = yv[core, side, 2 * extra :, at].astype(F32)
                scan_hat = yv[core, side, 2 * extra :, more].astype(F32)
                gelu_out[:, column] = gelu_hat * gain[...]
                scan_out[:, column] = scan_hat * gain[...]
                output_out[:, column] = wo[core, side, :, at].astype(F32)
                in_out[block, :, lanes] = yv[core, side, :extra, at].astype(F32)[:rows]
                de_out[block, :, lanes] = yv[core, side, :extra, more].astype(F32)[:rows]
                sums[...] += gelu_hat * gelu[:, column].astype(F32) + scan_hat * scan[
                    :, column
                ].astype(F32)


def unpacked_narrow(yv, wo, gain, gelu, scan, local_blocks, gate_rows, extra):
    part, width = gelu.shape
    gate = ((local_blocks, gate_rows, 2 * LANES), F32)
    return in_vmem(
        functools.partial(unpack_narrow, extra=extra),
        [yv, wo, gain, gelu, scan],
        [((part, width), F32)] * 3 + [gate, gate, ((part, LANES), F32)],
    )


def gelu_parts(w):
    inner = jnp.tanh(GELU_A * (w + GELU_B * w * w * w))
    return 0.5 * w * (1.0 + inner), inner


def gelu_slope(w, inner):
    return 0.5 * (1.0 + inner) + 0.5 * w * (1.0 - inner * inner) * GELU_A * (
        1.0 + 3.0 * GELU_B * w * w
    )


def rate_parts(ga, soft_row):
    log_rate = -8.0 * ga * soft_row
    twice = 2.0 * log_rate
    near = -twice * (
        1.0 + twice * (0.5 + twice * (1.0 / 6 + twice * (1.0 / 24 + twice * (1.0 / 120))))
    )
    rate = jnp.exp(log_rate)
    far = 1.0 - jnp.exp(twice)
    return rate, jnp.sqrt(jnp.where(twice > -0.1, near, far))


def filter_kernel(slot, yv, before, rows, y, vp, c, cb, *, th, taps):
    total, wide = y.shape
    vp[0:8, :] = before[...]

    def order(b, carry):
        block = yv[pl.ds(pl.multiple_of(slot[b] * th, th), th), :]
        y[pl.ds(pl.multiple_of(b * th, th), th), :] = block[:, :wide]
        vp[pl.ds(pl.multiple_of(b * th + 8, 8), th), :] = block[:, wide:]
        return carry

    lax.fori_loop(0, total // th, order, 0)

    def chunk(i, carry):
        start = pl.multiple_of(i * CHUNK, CHUNK)
        window = vp[pl.ds(start, CHUNK + 8), :]
        out = rows[0:1, :] * window[8 : 8 + CHUNK]
        for k in range(1, taps):
            out = out + rows[k : k + 1, :] * window[8 - k : 8 - k + CHUNK]
        c[pl.ds(start, CHUNK), :] = out
        cb[pl.ds(start, CHUNK), :] = out.astype(BF16)
        return carry

    lax.fori_loop(0, total // CHUNK, chunk, 0)


def put(ref, at, value):
    for i in range(ref.shape[0]):
        ref[i, at, :] = value[:, i * LANES : (i + 1) * LANES]


def got(ref, at):
    return jnp.concatenate([ref[i, at, :] for i in range(ref.shape[0])], axis=1)


def states_kernel(cb, far, whole, near_gates, far_gates, c, rows, gi, ga, hp, p, ends, pair, a):
    total, wide = c.shape
    length = total // 8
    bias_i, bias_a, soft = rows[0:1, :], rows[1:2, :], rows[2:3, :]

    def chunk(i, carry):
        at = pl.ds(pl.multiple_of(i * CHUNK, CHUNK), CHUNK)
        full = jnp.dot(cb[at, : 2 * LANES], whole[...], preferred_element_type=F32)
        half = jnp.dot(cb[at, 2 * LANES :], near_gates[...], preferred_element_type=F32)
        half = half + jnp.dot(far[at, :], far_gates[...], preferred_element_type=F32)
        pre_i = jnp.concatenate([full[:, : 2 * LANES], half[:, :LANES]], axis=1)
        pre_a = jnp.concatenate([full[:, 2 * LANES :], half[:, LANES:]], axis=1)
        open_i = jax.nn.sigmoid(pre_i + bias_i)
        open_a = jax.nn.sigmoid(pre_a + bias_a)
        rate, scale = rate_parts(open_a, soft)
        gi[at, :] = open_i
        ga[at, :] = open_a
        put(a, at, rate)
        put(hp, at, scale * open_i * c[at, :])
        return carry

    lax.fori_loop(0, total // CHUNK, chunk, 0)

    tiles = wide // LANES

    def step(t, carry):
        at = pl.ds(t, 8, stride=length)
        out = []
        for i, (h, q) in enumerate(carry):
            rate = a[i, at, :]
            h = rate * h + hp[i, at, :]
            q = q * rate
            hp[i, at, :] = h
            p[i, at, :] = q
            out.append((h, q))
        return tuple(out)

    start = ((jnp.zeros((8, LANES), F32), jnp.ones((8, LANES), F32)),) * tiles
    last, product = (
        jnp.concatenate(parts, axis=1)
        for parts in zip(*lax.fori_loop(0, length, step, start, unroll=8))
    )
    ends[0:8, :] = product
    ends[8:16, :] = last
    rates, state = product[0:1], last[0:1]
    for j in range(1, 8):
        state = product[j : j + 1] * state + last[j : j + 1]
        rates = rates * product[j : j + 1]
    pair[...] = jnp.zeros_like(pair)
    pair[0:1, :] = rates
    pair[1:2, :] = state


def merge_kernel(slot, hp, p, ends, carry_in, y, h, ob, *, th):
    total = y.shape[0]
    per = total // 8 // th
    enter = carry_in[...]
    h[0:8, :] = jnp.broadcast_to(enter, (8, enter.shape[1]))
    for j in range(8):

        def finish(i, carry, j=j, enter=enter):
            b = j * per + i
            at = pl.ds(pl.multiple_of(b * th, th), th)
            state = got(hp, at) + got(p, at) * enter
            h[pl.ds(pl.multiple_of(b * th + 8, 8), th), :] = state
            out, _ = gelu_parts(y[at, :])
            ob[pl.ds(pl.multiple_of(slot[b] * th, th), th), :] = (state * out).astype(BF16)
            return carry

        lax.fori_loop(0, per, finish, 0)
        enter = ends[8 + j : 9 + j, :] + ends[j : j + 1, :] * enter


def adjoint_kernel(slot, dob, y, h, ga, rows, dy, lam, q, ends, pair, a, *, th):
    total, wide = y.shape
    length = total // 8
    soft = rows[2:3, :]

    def order(b, carry):
        at = pl.ds(pl.multiple_of(b * th, th), th)
        there = pl.ds(pl.multiple_of(slot[b] * th, th), th)
        block = dob[there, :]
        w = y[at, :]
        out, inner = gelu_parts(w)
        put(lam, at, block * out)
        state = h[pl.ds(pl.multiple_of(b * th + 8, 8), th), :]
        dy[there, :] = (block * state * gelu_slope(w, inner)).astype(BF16)
        put(a, at, jnp.exp(-8.0 * ga[at, :] * soft))
        return carry

    lax.fori_loop(0, total // th, order, 0)

    tiles = wide // LANES

    def step(t, carry):
        at = pl.ds(length - 1 - t, 8, stride=length)
        out = []
        for i, (later, product) in enumerate(carry):
            here = lam[i, at, :] + later
            lam[i, at, :] = here
            q[i, at, :] = product
            rate = a[i, at, :]
            out.append((rate * here, product * rate))
        return tuple(out)

    start = ((jnp.zeros((8, LANES), F32), jnp.ones((8, LANES), F32)),) * tiles
    first, product = (
        jnp.concatenate(parts, axis=1)
        for parts in zip(*lax.fori_loop(0, length, step, start, unroll=8))
    )
    ends[0:8, :] = product
    ends[8:16, :] = first
    rates, state = product[7:8], first[7:8]
    for j in range(6, -1, -1):
        state = product[j : j + 1] * state + first[j : j + 1]
        rates = rates * product[j : j + 1]
    pair[...] = jnp.zeros_like(pair)
    pair[0:1, :] = rates
    pair[1:2, :] = state


def gates_kernel(lam, q, ends, carry_in, h, gi, ga, c, rows, dpi, dpa, dc, sums):
    total, wide = c.shape
    length = total // 8
    soft = rows[2:3, :]
    step = min(length, 64)
    enter = carry_in[...]
    carry = (jnp.zeros((1, wide), F32),) * 3
    for j in range(7, -1, -1):

        def finish(i, carry, j=j, enter=enter):
            start = pl.multiple_of(j * length + i * step, 8)
            at = pl.ds(start, step)
            state_grad = got(lam, at) + got(q, at) * enter
            before = h[pl.ds(start, step + 8), :][7 : 7 + step]
            open_i, open_a, filtered = gi[at, :], ga[at, :], c[at, :]
            rate, scale = rate_parts(open_a, soft)
            dla = state_grad * before * rate - state_grad * open_i * filtered * rate * rate / scale
            grad_i = state_grad * scale * filtered * open_i * (1.0 - open_i)
            slope = -8.0 * open_a * dla
            grad_a = soft * slope * (1.0 - open_a)
            dpi[at, :] = grad_i.astype(BF16)
            dpa[at, :] = grad_a.astype(BF16)
            dc[at, :] = state_grad * scale * open_i
            return (
                carry[0] + jnp.sum(grad_i, axis=0, keepdims=True),
                carry[1] + jnp.sum(grad_a, axis=0, keepdims=True),
                carry[2] + jnp.sum(slope, axis=0, keepdims=True),
            )

        carry = lax.fori_loop(0, length // step, finish, carry)
        enter = ends[8 + j : 9 + j, :] + ends[j : j + 1, :] * enter
    sums[...] = jnp.zeros_like(sums)
    for row in range(3):
        sums[row : row + 1, :] = carry[row]


def ungate_kernel(dpi, dpa, far, in_whole, de_whole, near_gates, far_gates, dc, vp, dcp, sums, *, taps):
    total = dc.shape[0]
    last = (((1,), (1,)), ((), ()))
    full, half = slice(0, 2 * LANES), slice(2 * LANES, 3 * LANES)
    turned = lambda left, right: lax.dot_general(left, right, last, preferred_element_type=F32)

    def chunk(i, carry):
        start = pl.multiple_of(i * CHUNK, CHUNK)
        at = pl.ds(start, CHUNK)
        whole = turned(dpi[at, full], in_whole[...]) + turned(dpa[at, full], de_whole[...])
        middle = (
            turned(dpi[at, half], near_gates[:, :LANES])
            + turned(dpa[at, half], near_gates[:, LANES:])
            + turned(far[at, :], far_gates[...])
        )
        out = dc[at, :] + jnp.concatenate([whole, middle], axis=1)
        dcp[at, :] = out
        window = vp[pl.ds(start, CHUNK + 8), :]
        return tuple(
            carry[k] + jnp.sum(out * window[8 - k : 8 - k + CHUNK], axis=0, keepdims=True)
            for k in range(taps)
        )

    zero = jnp.zeros((1, dc.shape[1]), F32)
    carry = lax.fori_loop(0, total // CHUNK, chunk, (zero,) * taps)
    sums[...] = jnp.zeros_like(sums)
    for k in range(taps):
        sums[k : k + 1, :] = carry[k]


def unfilter_kernel(slot, dc, following, rows, dv, dcp, *, th, taps):
    total = dc.shape[0]
    dcp[0:total, :] = dc[...]
    dcp[total : total + 8, :] = following[...]

    def order(b, carry):
        window = dcp[pl.ds(pl.multiple_of(b * th, th), th + 8), :]
        out = rows[0:1, :] * window[0:th]
        for k in range(1, taps):
            out = out + rows[k : k + 1, :] * window[k : k + th]
        dv[pl.ds(pl.multiple_of(slot[b] * th, th), th), :] = out.astype(BF16)
        return carry

    lax.fori_loop(0, total // th, order, 0)


def feed_kernel(ge, dz, zb, dge, *, th):
    lanes = dz.shape[1]

    def block(b, carry):
        at = pl.ds(pl.multiple_of(b * th, th), th)
        g, e, d = ge[at, :lanes], ge[at, lanes:], dz[at, :]
        act, inner = gelu_parts(g)
        zb[at, :] = (act * e).astype(BF16)
        dge[at, :lanes] = (d * e * gelu_slope(g, inner)).astype(BF16)
        dge[at, lanes:] = (d * act).astype(BF16)
        return carry

    lax.fori_loop(0, dz.shape[0] // th, block, 0)


def on_chip(kernel, slot, inputs, outs, scratch=()):
    vmem = pl.BlockSpec(memory_space=pltpu.VMEM)
    return pl.pallas_call(
        kernel,
        out_shape=[jax.ShapeDtypeStruct(shape, dtype) for shape, dtype in outs],
        in_specs=[pl.BlockSpec(memory_space=pltpu.SMEM)] + [vmem] * len(inputs),
        out_specs=[vmem] * len(outs),
        scratch_shapes=[pltpu.VMEM(shape, dtype) for shape, dtype in scratch],
        compiler_params=params(),
    )(slot, *inputs)


def in_vmem(kernel, inputs, outs, scratch=()):
    vmem = pl.BlockSpec(memory_space=pltpu.VMEM)
    return pl.pallas_call(
        kernel,
        out_shape=[jax.ShapeDtypeStruct(shape, dtype) for shape, dtype in outs],
        in_specs=[vmem] * len(inputs),
        out_specs=[vmem] * len(outs),
        scratch_shapes=[pltpu.VMEM(shape, dtype) for shape, dtype in scratch],
        compiler_params=params(),
    )(*inputs)


def dot(left, right, over):
    return lax.dot_general(left, right, (over, ((), ())), preferred_element_type=F32)


def shards(
    block_input,
    first_gain,
    gelu_weight,
    scan_weight,
    filter_taps,
    input_gate,
    input_bias,
    decay_gate,
    decay_bias,
    decay_param,
    output_weight,
    second_gain,
    expand_gate,
    expand_value,
    contract_weight,
    output_cotangent,
):
    count = lax.axis_size("seq")
    chip = lax.axis_index("seq")
    core = lax.axis_index("head")
    th = block_input.shape[0] // 2
    width = block_input.shape[1]
    part = gelu_weight.shape[0]
    taps = filter_taps.shape[0]
    local_blocks, gate_rows, block_width = input_gate.shape
    assert block_width == 2 * LANES and width == part * count and local_blocks == 5
    place = chip // 4
    fours = count // 4
    near = 8 * th
    total = 2 * count * th
    lanes_r = 3 * LANES
    slab = 4 * part

    hidden = expand_gate.shape[1]
    lanes = LANES * -(-hidden // (count * LANES))
    hidden_chips = hidden // lanes
    assert hidden_chips * lanes == hidden

    number = jnp.arange(8, dtype=jnp.int32)
    relative = (chip & 3) ^ (number // 2)
    turned = ((relative & 1) << 1) | (relative >> 1)
    slot = jnp.where(number % 2 == 0, turned, relative) + jnp.where(number % 2 == core, 0, 4)
    slot = slot.astype(jnp.int32)

    def slabs(rows):
        return jnp.concatenate(
            [lax.dynamic_slice_in_dim(rows, (place ^ j) * slab, slab, 1) for j in range(fours)],
            axis=1,
        )

    extra = max(16, gate_rows)
    more_rows = ((0, 0), (0, extra - gate_rows), (0, 0))
    gain1 = first_gain.astype(F32)[:, None]
    small = jnp.concatenate(
        [
            filter_taps.transpose(1, 0, 2),
            input_bias[:, None],
            decay_bias[:, None],
            decay_param[:, None],
        ],
        axis=1,
    )
    small = jnp.pad(
        small, ((0, 0), (0, extra - small.shape[1]), (0, LANES - small.shape[2]))
    )
    packed = packed_narrow(
        gain1,
        gelu_weight,
        scan_weight,
        output_weight.T,
        jnp.pad(input_gate, more_rows),
        jnp.pad(decay_gate, more_rows),
        small,
    )

    def both_sides(pieces):
        kept = lax.dynamic_index_in_dim(pieces, core, 0, False)
        given = core_swap(lax.dynamic_index_in_dim(pieces, 1 - core, 0, False))
        return jnp.concatenate(
            [jnp.where(core == 0, kept, given), jnp.where(core == 0, given, kept)], axis=0
        )

    packed = [near_exchanged(both_sides(piece)) for piece in packed]
    pieces_yv = row_gathered(packed[0])
    weight_yv = jnp.concatenate([piece[:, 2 * extra :].reshape(slab, -1) for piece in pieces_yv])
    heads = jnp.stack([piece[:, : 2 * extra] for piece in pieces_yv])
    heads = jnp.concatenate(
        [lax.dynamic_index_in_dim(heads, place ^ j, 0, False) for j in range(fours)]
    )
    gates = heads[:, :gate_rows].reshape(block_width, 2 * lanes_r)
    small = heads[:, extra : extra + taps + 3]
    small = [
        small[:, :, i * LANES : i * LANES + gate_rows].transpose(1, 0, 2).reshape(taps + 3, -1)
        for i in range(2)
    ]
    own_half = lambda a, axis=0: lax.dynamic_slice_in_dim(a, core * LANES, LANES, axis)
    far_half = lambda a, axis=0: lax.dynamic_slice_in_dim(a, (1 - core) * LANES, LANES, axis)
    small = jnp.concatenate([small[0], own_half(small[1], 1)], axis=1).astype(F32)
    tap_rows = jnp.pad(small[:taps], ((0, 8 - taps), (0, 0)))
    param_row = small[taps + 2 :]
    gate_rows_of = jnp.pad(
        jnp.concatenate([small[taps : taps + 2], jax.nn.softplus(param_row)], axis=0),
        ((0, 5), (0, 0)),
    )
    in_whole, de_whole = gates[:, : 2 * LANES], gates[:, lanes_r : lanes_r + 2 * LANES]
    half_gates = jnp.concatenate([gates[:, 2 * LANES : lanes_r], gates[:, lanes_r + 2 * LANES :]], 1)

    x = lax.dynamic_slice_in_dim(block_input, core * th, th, 0).astype(F32)
    s1 = lax.rsqrt(jnp.mean(x * x, axis=-1, keepdims=True) + EPSILON)
    first = near_gathered(slabs((x * s1).astype(BF16)))
    cotangent = lax.dynamic_slice_in_dim(output_cotangent, core * th, th, 0)
    given_out = jnp.concatenate(gathered(after(cotangent, first)))
    pieces_out = row_gathered(after(packed[1], *pieces_yv))
    weight_out = jnp.concatenate([piece.reshape(slab, lanes_r) for piece in pieces_out])

    gain2 = second_gain.astype(F32)[:, None]
    wide = packed_wide(gain2, expand_gate, expand_value, contract_weight.T, count, lanes)
    wide = all_to_all(after(wide, weight_yv)).reshape(width, 3 * lanes)

    yv = dot(first, weight_yv, ((1,), (0,)))
    tail = lax.dynamic_slice_in_dim(yv[:, lanes_r:], slot[7] * th + th - 8, 8, 0)
    token_f32, token_bf16 = ((near, lanes_r), F32), ((near, lanes_r), BF16)
    padded = ((near + 8, lanes_r), F32)
    few = ((8, lanes_r), F32)
    tiled = ((3, near, LANES), F32)
    y, vp, c, cb = on_chip(
        functools.partial(filter_kernel, th=th, taps=taps),
        slot,
        [yv, next_four(tail, 1), tap_rows],
        [token_f32, padded, token_f32, token_bf16],
    )
    cb_far = core_swap(cb[:, 2 * LANES :])
    near_gates, far_gates = own_half(half_gates), far_half(half_gates)
    gi, ga, hp, p, ends, pair = in_vmem(
        states_kernel,
        [
            cb,
            cb_far,
            jnp.concatenate([in_whole, de_whole], axis=1),
            near_gates,
            far_gates,
            c,
            gate_rows_of,
        ],
        [token_f32, token_f32, tiled, tiled, ((16, lanes_r), F32), few],
        [tiled],
    )
    h, ob = on_chip(
        functools.partial(merge_kernel, th=th),
        slot,
        [hp, p, ends, carried(pair, place, False), y],
        [padded, token_bf16],
    )
    weight_ge, weight_c = wide[:, : 2 * lanes], wide[:, 2 * lanes :]
    dz = dot(given_out, weight_c, ((1,), (0,)))
    out_both = jnp.concatenate([weight_out, core_swap(weight_out)], axis=1)
    r = x + slabs(near_scattered(ob, out_both))

    s2 = lax.rsqrt(jnp.mean(r * r, axis=-1, keepdims=True) + EPSILON)
    second = gathered((r * s2).astype(BF16), [dz])
    second = jnp.concatenate(second)
    zb, dge = in_vmem(
        functools.partial(feed_kernel, th=th),
        [dot(second, weight_ge, ((1,), (0,))), dz],
        [((total, lanes), BF16), ((total, 2 * lanes), BF16)],
    )
    ge_both = jnp.concatenate([weight_ge, core_swap(weight_ge)], axis=1)
    c_both = jnp.concatenate([weight_c, core_swap(weight_c)], axis=1)
    (back2,) = scattered((grouped(dge), ge_both))
    dr = (
        cotangent.astype(F32)
        + s2 * back2
        - r * (s2 * s2 * s2) * jnp.mean(back2 * r, axis=-1, keepdims=True)
    )
    wide_grad, turned_grad = (
        dot(second, dge, ((0,), (0,))).astype(BF16).reshape(count, part, 2 * lanes),
        dot(given_out, zb, ((0,), (0,))).astype(BF16).reshape(count, part, lanes),
    )
    wide_grad, turned_grad = lax.optimization_barrier((wide_grad, turned_grad))
    turned_grad = all_to_all(turned_grad)
    dq = after(near_gathered(slabs(dr.astype(BF16))), turned_grad)
    dq, wide_grad = lax.optimization_barrier((dq, wide_grad))
    (out_sum,) = scattered((grouped(after(zb, dq)), c_both))
    out_half = (r + out_sum).astype(BF16)
    wide_grad = all_to_all(wide_grad)
    gate_grad_out, value_grad_out, contract_grad_out, gain2_part = unpacked_wide(
        wide_grad, turned_grad, gain2, expand_gate, expand_value, lanes
    )

    dob = dot(dq, weight_out, ((1,), (0,)))
    dy, lam, q, ends, pair = on_chip(
        functools.partial(adjoint_kernel, th=th),
        slot,
        [dob, y, h, ga, gate_rows_of],
        [token_bf16, tiled, tiled, ((16, lanes_r), F32), few],
        [tiled],
    )
    dpi, dpa, dc, sums = in_vmem(
        gates_kernel,
        [lam, q, ends, carried(pair, place, True), h, gi, ga, c, gate_rows_of],
        [token_bf16, token_bf16, token_f32, few],
    )
    half_grads = jnp.concatenate([dpi[:, 2 * LANES :], dpa[:, 2 * LANES :]], axis=1)
    dc, tap_sums = in_vmem(
        functools.partial(ungate_kernel, taps=taps),
        [
            dpi,
            dpa,
            core_swap(half_grads),
            in_whole,
            de_whole,
            near_gates,
            own_half(core_swap(half_gates)),
            dc,
            vp,
        ],
        [token_f32, few],
    )
    dv = on_chip(
        functools.partial(unfilter_kernel, th=th, taps=taps),
        slot,
        [dc, next_four(dc[:8], -1), tap_rows],
        [token_bf16],
        [padded],
    )[0]
    dyv = jnp.concatenate([dy, dv], axis=1)

    def to_owners(grad):
        grad = row_scattered(list(grad)).astype(BF16)
        grad = near_exchanged(grad)
        kept = lax.dynamic_slice_in_dim(grad, 2 * core, 2, 0)
        given = core_swap(lax.dynamic_slice_in_dim(grad, 2 * (1 - core), 2, 0))
        return jnp.stack([jnp.where(core == 0, kept, given), jnp.where(core == 0, given, kept)])

    out_grad = lax.optimization_barrier(dot(dq, ob, ((0,), (0,))).astype(BF16))
    out_grad = to_owners(out_grad.reshape(fours, 4, part, lanes_r))
    yv_grad = lax.optimization_barrier(dot(first, dyv, ((0,), (0,))).astype(BF16))
    yv_grad = yv_grad.reshape(fours, 4, part, 2 * lanes_r)

    def gate_grad(grad):
        whole = dot(cb[:, : 2 * LANES], grad[:, : 2 * LANES], ((0,), (0,)))
        own_rows = dot(cb[:, 2 * LANES :], grad[:, 2 * LANES :], ((0,), (0,)))
        far_rows = dot(cb_far, grad[:, 2 * LANES :], ((0,), (0,)))
        half = jnp.concatenate(
            [jnp.where(core == 0, own_rows, far_rows), jnp.where(core == 0, far_rows, own_rows)]
        )
        return jnp.concatenate([whole, half], axis=1)

    head_grad = jnp.concatenate([gate_grad(dpi), gate_grad(dpa)], axis=1)
    head_grad = head_grad.reshape(count, gate_rows, 2 * lanes_r)
    head_grad = jnp.pad(head_grad, ((0, 0), (0, extra - gate_rows), (0, 0)))
    small_grad = jnp.concatenate(
        [tap_sums[:taps], sums[:2], sums[2:3] * jax.nn.sigmoid(param_row)], axis=0
    )
    middle = small_grad[:, 2 * LANES :]
    nothing = jnp.zeros_like(middle)
    small_grad = [
        small_grad[:, : 2 * LANES],
        jnp.where(
            core == 0,
            jnp.concatenate([middle, nothing], axis=1),
            jnp.concatenate([nothing, middle], axis=1),
        ),
    ]
    small_grad = [
        jnp.pad(
            a.reshape(taps + 3, count, gate_rows).transpose(1, 0, 2),
            ((0, 0), (0, extra - taps - 3), (0, LANES - gate_rows)),
        )
        for a in small_grad
    ]
    small_grad = jnp.concatenate(small_grad, axis=2)
    small_grad = jnp.pad(small_grad, ((0, 0), (0, 0), (0, 2 * lanes_r - 2 * LANES)))
    head_grad = jnp.concatenate([head_grad, small_grad], axis=1).astype(BF16)
    head_grad = head_grad.reshape(fours, 4, 2 * extra, 2 * lanes_r)
    head_grad = jnp.stack(
        [lax.dynamic_index_in_dim(head_grad, place ^ j, 0, False) for j in range(fours)]
    )
    yv_grad = to_owners(jnp.concatenate([head_grad, yv_grad], axis=2))
    (
        gelu_grad_out,
        scan_grad_out,
        output_grad_out,
        input_gate_out,
        decay_gate_out,
        gain1_part,
    ) = unpacked_narrow(
        yv_grad, out_grad, gain1, gelu_weight, scan_weight, local_blocks, gate_rows, extra
    )
    small_sum = yv_grad[:, :, extra : extra + taps + 3].astype(F32)
    whole_sum = small_sum[..., :gate_rows]
    half_sum = small_sum[..., LANES : LANES + gate_rows]
    half_sum = half_sum[0] + half_sum[1]
    small_sum = jnp.stack(
        [whole_sum[0, 0], half_sum[0], whole_sum[1, 0], whole_sum[0, 1], whole_sum[1, 1]], axis=1
    )

    back1 = slabs(near_scattered(dyv, weight_yv, core_swap(weight_yv)))
    in_half = dr + s1 * back1 - x * (s1 * s1 * s1) * jnp.mean(back1 * x, axis=-1, keepdims=True)

    gain_parts = jnp.stack([jnp.sum(gain1_part, axis=1), jnp.sum(gain2_part, axis=1)])
    gain_grads = gain_parts + core_swap(gain_parts)

    def both_halves(half):
        swapped = core_swap(half)
        return jnp.concatenate(
            [jnp.where(core == 0, half, swapped), jnp.where(core == 0, swapped, half)], axis=0
        )

    return (
        both_halves(out_half),
        both_halves(in_half),
        gain_grads[0],
        gelu_grad_out,
        scan_grad_out,
        small_sum[:taps],
        input_gate_out,
        small_sum[taps],
        decay_gate_out,
        small_sum[taps + 1],
        small_sum[taps + 2],
        output_grad_out.T,
        gain_grads[1],
        gate_grad_out,
        value_grad_out,
        contract_grad_out.T,
    )


def solution(mesh):
    in_specs = (
        P("seq", None),
        P("seq"),
        P("seq", "head"),
        P("seq", "head"),
        P(None, "head", "seq"),
        P("head", "seq", None),
        P("head", "seq"),
        P("head", "seq", None),
        P("head", "seq"),
        P("head", "seq"),
        P("head", "seq"),
        P("seq"),
        P("seq", "head"),
        P("seq", "head"),
        P("head", "seq"),
        P("seq", None),
    )
    out_specs = (
        P("seq", None),
        P("seq", None),
        P("seq"),
        P("seq", "head"),
        P("seq", "head"),
        P(None, "head", "seq"),
        P("head", "seq", None),
        P("head", "seq"),
        P("head", "seq", None),
        P("head", "seq"),
        P("head", "seq"),
        P("head", "seq"),
        P("seq"),
        P("seq", "head"),
        P("seq", "head"),
        P("head", "seq"),
    )
    return jax.shard_map(shards, mesh=mesh, in_specs=in_specs, out_specs=out_specs, check_vma=False)
```

```python
import functools

import jax
import jax.numpy as jnp
from jax import lax
from jax.experimental import pallas as pl
from jax.experimental.pallas import tpu as pltpu
from jax.sharding import PartitionSpec as P

BF16 = jnp.bfloat16
F32 = jnp.float32
EPSILON = 1e-06
BOTH = ("seq", "head")
LANES = 128
CHUNK = 128
GELU_A = 0.7978845608028654
GELU_B = 0.044715
VMEM_BYTES = 56 * 1024 * 1024


def xor_send(value, mask_first, mask_second=None, allowed=None):
    count = lax.axis_size("seq")
    masks = (mask_first, mask_first if mask_second is None else mask_second)
    pairs = [
        (chip * 2 + core, (chip ^ masks[core]) * 2 + core)
        for chip in range(count)
        for core in range(2)
        if allowed is None or allowed(chip, chip ^ masks[core])
    ]
    return lax.ppermute(value, BOTH, pairs)


def core_swap(value):
    return lax.ppermute(value, "head", [(0, 1), (1, 0)])


def row_send(value, to):
    pairs = [
        (row * 8 + device, to[row] * 8 + device) for row in sorted(to) for device in range(8)
    ]
    return lax.ppermute(value, BOTH, pairs)


PAIRED = {0: 1, 1: 0, 2: 3, 3: 2}
CROSSED = {1: 2, 2: 1}
OUTWARD = {1: 0, 2: 3}


def row_gathered(rows):
    count = lax.axis_size("seq")
    if count != 16:
        return [rows] + [xor_send(rows, 4 * g) for g in range(1, count // 4)]
    one = row_send(rows, PAIRED)
    cross = row_send(rows, CROSSED)
    far = row_send(one, CROSSED)
    return [rows, one, far + row_send(cross, OUTWARD), cross + row_send(far, OUTWARD)]


def gathered(rows, early=()):
    own = []
    columns = row_gathered(rows)
    for g, block in enumerate(columns):
        pair = jnp.concatenate([block, xor_send(block, 2, 1)], axis=0)
        if g == len(columns) - 1 and early:
            pair = after(pair, *early)
        own.append(jnp.concatenate([pair, xor_send(pair, 1, 2)], axis=0))
    return own + [core_swap(group) for group in own]


def scattered(*products):
    count = lax.axis_size("seq") // 4
    rows = products[0][0][0].shape[0] // 4
    parts = len(products)

    def sent(arrays, *masks):
        moved = xor_send(jnp.concatenate([a.astype(BF16) for a in arrays]), *masks)
        return [a.astype(F32) for a in jnp.split(moved, parts)]

    own = None
    arriving = []
    for g in list(range(1, count)) + [0]:
        sums = [dot(groups[g], right, ((1,), (1,))).astype(BF16) for groups, right in products]
        more = sent([a[2 * rows :] for a in sums], 1, 2)
        sums = [a[: 2 * rows].astype(F32) + b for a, b in zip(sums, more)]
        more = sent([a[rows:] for a in sums], 2, 1)
        sums = [a[:rows] + b for a, b in zip(sums, more)]
        if g:
            arriving.append(sent(sums, 4 * g))
        else:
            own = sums
    for more in arriving:
        own = [a + b for a, b in zip(own, more)]
    return own


INWARD = {0: 1, 3: 2}


def row_scattered(parts):
    own = parts[0].astype(F32)
    if len(parts) != 4:
        moved = [xor_send(part, 4 * g).astype(F32) for g, part in enumerate(parts) if g]
        return functools.reduce(jnp.add, moved, own)
    _, one, two, three = parts
    two, three = (
        two.astype(F32) + row_send(three, INWARD).astype(F32),
        three.astype(F32) + row_send(two, INWARD).astype(F32),
    )
    own = own + row_send(three.astype(BF16), CROSSED).astype(F32)
    one = one.astype(F32) + row_send(two.astype(BF16), CROSSED).astype(F32)
    return own + row_send(one.astype(BF16), PAIRED).astype(F32)


def near_gathered(rows):
    pair = jnp.concatenate([rows, xor_send(rows, 2, 1)], axis=0)
    own = jnp.concatenate([pair, xor_send(pair, 1, 2)], axis=0)
    return jnp.concatenate([own, core_swap(own)], axis=0)


def near_scattered(rows, *right):
    half = rows.shape[0] // 2
    th = half // 4
    both = (rows[:half], core_swap(rows[half:]))
    if len(right) == 1:
        both = (jnp.concatenate(both, axis=1),)
    partial = sum(dot(a, b, ((1,), (1,))) for a, b in zip(both, right)).astype(BF16)
    pair = partial[: 2 * th].astype(F32) + xor_send(partial[2 * th :], 1, 2).astype(F32)
    return pair[:th] + xor_send(pair[th:].astype(BF16), 2, 1).astype(F32)


def near_exchanged(pieces):
    count = lax.axis_size("seq")
    fours = [list(range(first, first + 4)) for first in range(0, count, 4)]
    return lax.all_to_all(pieces, "seq", 0, 0, tiled=True, axis_index_groups=fours)


def next_four(value, step):
    count = lax.axis_size("seq")
    pairs = [
        (chip * 2 + core, (chip + 4 * step) * 2 + core)
        for chip in range(count)
        for core in range(2)
        if 0 <= chip + 4 * step < count
    ]
    return lax.ppermute(value, BOTH, pairs)


def carried(pair, place, reverse):
    count = lax.axis_size("seq") // 4
    pairs = jnp.stack([pair] + [xor_send(pair, 4 * g) for g in range(1, count)])
    state = jnp.zeros_like(pair[:1])
    for lap in range(count - 1):
        source = count - 1 - lap if reverse else lap
        one = lax.dynamic_index_in_dim(pairs, place ^ source, 0, False)
        ahead = source > place if reverse else source < place
        state = jnp.where(ahead, one[0:1] * state + one[1:2], state)
    return state


def grouped(rows):
    half = rows.shape[0] // 2
    both = jnp.concatenate([rows[:half], core_swap(rows[half:])], axis=1)
    return list(both.reshape(lax.axis_size("seq") // 4, -1, both.shape[1]))


def after(value, *others):
    return lax.optimization_barrier((value,) + others)[0]


def all_to_all(pieces):
    return lax.all_to_all(pieces, "seq", 0, 0, tiled=True)


def params(**more):
    return pltpu.CompilerParams(vmem_limit_bytes=VMEM_BYTES, **more)


def pack_wide(gain, gate, value, contract, out, *, chips):
    lanes = gate.shape[1]
    live = pl.program_id(0) < chips
    scale = jnp.where(live, gain[...], 0.0)
    out[0, :, :lanes] = (gate[...].astype(F32) * scale).astype(BF16)
    out[0, :, lanes : 2 * lanes] = (value[...].astype(F32) * scale).astype(BF16)
    out[0, :, 2 * lanes :] = jnp.where(live, contract[...].astype(F32), 0.0).astype(BF16)


def packed_wide(gain, gate, value, contract, count, lanes):
    part, hidden = gate.shape
    chips = hidden // lanes
    column = pl.BlockSpec((part, lanes), lambda j: (0, jnp.minimum(j, chips - 1)))
    return pl.pallas_call(
        functools.partial(pack_wide, chips=chips),
        out_shape=jax.ShapeDtypeStruct((count, part, 3 * lanes), BF16),
        grid=(count,),
        in_specs=[
            pl.BlockSpec((part, 1), lambda j: (0, 0)),
            column,
            column,
            column,
        ],
        out_specs=pl.BlockSpec((1, part, 3 * lanes), lambda j: (j, 0, 0)),
        compiler_params=params(),
    )(gain, gate, value, contract)


def unpack_wide(grads, turned, gain, gate, value, gate_out, value_out, contract_out, sums):
    lanes = gate.shape[1] // grads.shape[0]

    @pl.when(pl.program_id(0) == 0)
    def _():
        sums[...] = jnp.zeros_like(sums)

    total = sums[...]
    for i in range(grads.shape[0]):
        at = slice(i * lanes, (i + 1) * lanes)
        gate_hat = grads[i, :, :lanes].astype(F32)
        value_hat = grads[i, :, lanes : 2 * lanes].astype(F32)
        gate_out[:, at] = gate_hat * gain[...]
        value_out[:, at] = value_hat * gain[...]
        contract_out[:, at] = turned[i].astype(F32)
        both = gate_hat * gate[:, at].astype(F32) + value_hat * value[:, at].astype(F32)
        for start in range(0, lanes, LANES):
            total = total + both[:, start : start + LANES]
    sums[...] = total


def unpacked_wide(grads, turned, gain, gate, value, lanes):
    part, hidden = gate.shape
    chips = hidden // lanes
    at_once = 3 if chips % 3 == 0 else 1
    column = pl.BlockSpec((part, at_once * lanes), lambda j: (0, j))
    return pl.pallas_call(
        unpack_wide,
        out_shape=[
            jax.ShapeDtypeStruct((part, hidden), F32),
            jax.ShapeDtypeStruct((part, hidden), F32),
            jax.ShapeDtypeStruct((part, hidden), F32),
            jax.ShapeDtypeStruct((part, LANES), F32),
        ],
        grid=(chips // at_once,),
        in_specs=[
            pl.BlockSpec((at_once, part, 2 * lanes), lambda j: (j, 0, 0)),
            pl.BlockSpec((at_once, part, lanes), lambda j: (j, 0, 0)),
            pl.BlockSpec((part, 1), lambda j: (0, 0)),
            column,
            column,
        ],
        out_specs=[
            column,
            column,
            column,
            pl.BlockSpec((part, LANES), lambda j: (0, 0)),
        ],
        compiler_params=params(),
    )(grads, turned, gain, gate, value)


HALVES = (((0, 1, 2), (4, 5, 3)), ((6, 7, None), (8, 9, None)))


def pack_narrow(gain, gelu, scan, output, in_gate, de_gate, small, yv_out, wo_out, *, extra):
    for core in range(2):
        for side in range(2):
            halves = HALVES[side][core]
            few = yv_out.at[core, side, extra : 2 * extra, :]
            few[...] = jnp.zeros_like(few)
            for place, half in enumerate(halves):
                at = slice(place * LANES, (place + 1) * LANES)
                more = slice((3 + place) * LANES, (4 + place) * LANES)
                if half is None:
                    yv_out[core, side, :, at] = jnp.zeros_like(yv_out[core, side, :, at])
                    yv_out[core, side, :, more] = jnp.zeros_like(yv_out[core, side, :, more])
                    wo_out[core, side, :, at] = jnp.zeros_like(wo_out[core, side, :, at])
                    continue
                block, odd = half // 2, half % 2
                column = slice(half * LANES, (half + 1) * LANES)
                lanes = slice(odd * LANES, (odd + 1) * LANES)
                yv_out[core, side, :extra, at] = in_gate[block, :, lanes]
                yv_out[core, side, :extra, more] = de_gate[block, :, lanes]
                if place != 1:
                    spot = slice((place // 2) * LANES, (place // 2 + 1) * LANES)
                    yv_out[core, side, extra : 2 * extra, spot] = small[block]
                yv_out[core, side, 2 * extra :, at] = (
                    gelu[:, column].astype(F32) * gain[...]
                ).astype(BF16)
                yv_out[core, side, 2 * extra :, more] = (
                    scan[:, column].astype(F32) * gain[...]
                ).astype(BF16)
                wo_out[core, side, :, at] = output[:, column]


def packed_narrow(gain, gelu, scan, output, in_gate, de_gate, small):
    part = gelu.shape[0]
    extra = small.shape[1]
    return in_vmem(
        functools.partial(pack_narrow, extra=extra),
        [gain, gelu, scan, output, in_gate, de_gate, small],
        [((2, 2, 2 * extra + part, 6 * LANES), BF16), ((2, 2, part, 3 * LANES), BF16)],
    )


def unpack_narrow(
    yv, wo, gain, gelu, scan, gelu_out, scan_out, output_out, in_out, de_out, sums, *, extra
):
    rows = in_out.shape[1]
    sums[...] = jnp.zeros_like(sums)
    for core in range(2):
        for side in range(2):
            for place, half in enumerate(HALVES[side][core]):
                if half is None:
                    continue
                block, odd = half // 2, half % 2
                at = slice(place * LANES, (place + 1) * LANES)
                more = slice((3 + place) * LANES, (4 + place) * LANES)
                column = slice(half * LANES, (half + 1) * LANES)
                lanes = slice(odd * LANES, (odd + 1) * LANES)
                gelu_hat = yv[core, side, 2 * extra :, at].astype(F32)
                scan_hat = yv[core, side, 2 * extra :, more].astype(F32)
                gelu_out[:, column] = gelu_hat * gain[...]
                scan_out[:, column] = scan_hat * gain[...]
                output_out[:, column] = wo[core, side, :, at].astype(F32)
                in_out[block, :, lanes] = yv[core, side, :extra, at].astype(F32)[:rows]
                de_out[block, :, lanes] = yv[core, side, :extra, more].astype(F32)[:rows]
                sums[...] += gelu_hat * gelu[:, column].astype(F32) + scan_hat * scan[
                    :, column
                ].astype(F32)


def unpacked_narrow(yv, wo, gain, gelu, scan, local_blocks, gate_rows, extra):
    part, width = gelu.shape
    gate = ((local_blocks, gate_rows, 2 * LANES), F32)
    return in_vmem(
        functools.partial(unpack_narrow, extra=extra),
        [yv, wo, gain, gelu, scan],
        [((part, width), F32)] * 3 + [gate, gate, ((part, LANES), F32)],
    )


def gelu_parts(w):
    inner = jnp.tanh(GELU_A * (w + GELU_B * w * w * w))
    return 0.5 * w * (1.0 + inner), inner


def gelu_slope(w, inner):
    return 0.5 * (1.0 + inner) + 0.5 * w * (1.0 - inner * inner) * GELU_A * (
        1.0 + 3.0 * GELU_B * w * w
    )


def rate_parts(ga, soft_row):
    log_rate = -8.0 * ga * soft_row
    twice = 2.0 * log_rate
    near = -twice * (
        1.0 + twice * (0.5 + twice * (1.0 / 6 + twice * (1.0 / 24 + twice * (1.0 / 120))))
    )
    rate = jnp.exp(log_rate)
    far = 1.0 - jnp.exp(twice)
    return rate, jnp.sqrt(jnp.where(twice > -0.1, near, far))


def filter_kernel(slot, yv, before, rows, y, vp, c, cb, *, th, taps):
    total, wide = y.shape
    vp[0:8, :] = before[...]

    def order(b, carry):
        block = yv[pl.ds(pl.multiple_of(slot[b] * th, th), th), :]
        y[pl.ds(pl.multiple_of(b * th, th), th), :] = block[:, :wide]
        vp[pl.ds(pl.multiple_of(b * th + 8, 8), th), :] = block[:, wide:]
        return carry

    lax.fori_loop(0, total // th, order, 0)

    def chunk(i, carry):
        start = pl.multiple_of(i * CHUNK, CHUNK)
        window = vp[pl.ds(start, CHUNK + 8), :]
        out = rows[0:1, :] * window[8 : 8 + CHUNK]
        for k in range(1, taps):
            out = out + rows[k : k + 1, :] * window[8 - k : 8 - k + CHUNK]
        c[pl.ds(start, CHUNK), :] = out
        cb[pl.ds(start, CHUNK), :] = out.astype(BF16)
        return carry

    lax.fori_loop(0, total // CHUNK, chunk, 0)


def put(ref, at, value):
    for i in range(ref.shape[0]):
        ref[i, at, :] = value[:, i * LANES : (i + 1) * LANES]


def got(ref, at):
    return jnp.concatenate([ref[i, at, :] for i in range(ref.shape[0])], axis=1)


def states_kernel(cb, far, whole, near_gates, far_gates, c, rows, gi, ga, hp, p, ends, pair, a):
    total, wide = c.shape
    length = total // 8
    bias_i, bias_a, soft = rows[0:1, :], rows[1:2, :], rows[2:3, :]

    def chunk(i, carry):
        at = pl.ds(pl.multiple_of(i * CHUNK, CHUNK), CHUNK)
        full = jnp.dot(cb[at, : 2 * LANES], whole[...], preferred_element_type=F32)
        half = jnp.dot(cb[at, 2 * LANES :], near_gates[...], preferred_element_type=F32)
        half = half + jnp.dot(far[at, :], far_gates[...], preferred_element_type=F32)
        pre_i = jnp.concatenate([full[:, : 2 * LANES], half[:, :LANES]], axis=1)
        pre_a = jnp.concatenate([full[:, 2 * LANES :], half[:, LANES:]], axis=1)
        open_i = jax.nn.sigmoid(pre_i + bias_i)
        open_a = jax.nn.sigmoid(pre_a + bias_a)
        rate, scale = rate_parts(open_a, soft)
        gi[at, :] = open_i
        ga[at, :] = open_a
        put(a, at, rate)
        put(hp, at, scale * open_i * c[at, :])
        return carry

    lax.fori_loop(0, total // CHUNK, chunk, 0)

    tiles = wide // LANES

    def step(t, carry):
        at = pl.ds(t, 8, stride=length)
        out = []
        for i, (h, q) in enumerate(carry):
            rate = a[i, at, :]
            h = rate * h + hp[i, at, :]
            q = q * rate
            hp[i, at, :] = h
            p[i, at, :] = q
            out.append((h, q))
        return tuple(out)

    start = ((jnp.zeros((8, LANES), F32), jnp.ones((8, LANES), F32)),) * tiles
    last, product = (
        jnp.concatenate(parts, axis=1)
        for parts in zip(*lax.fori_loop(0, length, step, start, unroll=8))
    )
    ends[0:8, :] = product
    ends[8:16, :] = last
    rates, state = product[0:1], last[0:1]
    for j in range(1, 8):
        state = product[j : j + 1] * state + last[j : j + 1]
        rates = rates * product[j : j + 1]
    pair[...] = jnp.zeros_like(pair)
    pair[0:1, :] = rates
    pair[1:2, :] = state


def merge_kernel(slot, hp, p, ends, carry_in, y, h, ob, *, th):
    total = y.shape[0]
    per = total // 8 // th
    enter = carry_in[...]
    h[0:8, :] = jnp.broadcast_to(enter, (8, enter.shape[1]))
    for j in range(8):

        def finish(i, carry, j=j, enter=enter):
            b = j * per + i
            at = pl.ds(pl.multiple_of(b * th, th), th)
            state = got(hp, at) + got(p, at) * enter
            h[pl.ds(pl.multiple_of(b * th + 8, 8), th), :] = state
            out, _ = gelu_parts(y[at, :])
            ob[pl.ds(pl.multiple_of(slot[b] * th, th), th), :] = (state * out).astype(BF16)
            return carry

        lax.fori_loop(0, per, finish, 0)
        enter = ends[8 + j : 9 + j, :] + ends[j : j + 1, :] * enter


def adjoint_kernel(slot, dob, y, h, ga, rows, dy, lam, q, ends, pair, a, *, th):
    total, wide = y.shape
    length = total // 8
    soft = rows[2:3, :]

    def order(b, carry):
        at = pl.ds(pl.multiple_of(b * th, th), th)
        there = pl.ds(pl.multiple_of(slot[b] * th, th), th)
        block = dob[there, :]
        w = y[at, :]
        out, inner = gelu_parts(w)
        put(lam, at, block * out)
        state = h[pl.ds(pl.multiple_of(b * th + 8, 8), th), :]
        dy[there, :] = (block * state * gelu_slope(w, inner)).astype(BF16)
        put(a, at, jnp.exp(-8.0 * ga[at, :] * soft))
        return carry

    lax.fori_loop(0, total // th, order, 0)

    tiles = wide // LANES

    def step(t, carry):
        at = pl.ds(length - 1 - t, 8, stride=length)
        out = []
        for i, (later, product) in enumerate(carry):
            here = lam[i, at, :] + later
            lam[i, at, :] = here
            q[i, at, :] = product
            rate = a[i, at, :]
            out.append((rate * here, product * rate))
        return tuple(out)

    start = ((jnp.zeros((8, LANES), F32), jnp.ones((8, LANES), F32)),) * tiles
    first, product = (
        jnp.concatenate(parts, axis=1)
        for parts in zip(*lax.fori_loop(0, length, step, start, unroll=8))
    )
    ends[0:8, :] = product
    ends[8:16, :] = first
    rates, state = product[7:8], first[7:8]
    for j in range(6, -1, -1):
        state = product[j : j + 1] * state + first[j : j + 1]
        rates = rates * product[j : j + 1]
    pair[...] = jnp.zeros_like(pair)
    pair[0:1, :] = rates
    pair[1:2, :] = state


def gates_kernel(lam, q, ends, carry_in, h, gi, ga, c, rows, dpi, dpa, dc, sums):
    total, wide = c.shape
    length = total // 8
    soft = rows[2:3, :]
    step = min(length, 64)
    enter = carry_in[...]
    carry = (jnp.zeros((1, wide), F32),) * 3
    for j in range(7, -1, -1):

        def finish(i, carry, j=j, enter=enter):
            start = pl.multiple_of(j * length + i * step, 8)
            at = pl.ds(start, step)
            state_grad = got(lam, at) + got(q, at) * enter
            before = h[pl.ds(start, step + 8), :][7 : 7 + step]
            open_i, open_a, filtered = gi[at, :], ga[at, :], c[at, :]
            rate, scale = rate_parts(open_a, soft)
            dla = state_grad * before * rate - state_grad * open_i * filtered * rate * rate / scale
            grad_i = state_grad * scale * filtered * open_i * (1.0 - open_i)
            slope = -8.0 * open_a * dla
            grad_a = soft * slope * (1.0 - open_a)
            dpi[at, :] = grad_i.astype(BF16)
            dpa[at, :] = grad_a.astype(BF16)
            dc[at, :] = state_grad * scale * open_i
            return (
                carry[0] + jnp.sum(grad_i, axis=0, keepdims=True),
                carry[1] + jnp.sum(grad_a, axis=0, keepdims=True),
                carry[2] + jnp.sum(slope, axis=0, keepdims=True),
            )

        carry = lax.fori_loop(0, length // step, finish, carry)
        enter = ends[8 + j : 9 + j, :] + ends[j : j + 1, :] * enter
    sums[...] = jnp.zeros_like(sums)
    for row in range(3):
        sums[row : row + 1, :] = carry[row]


def ungate_kernel(dpi, dpa, far, in_whole, de_whole, near_gates, far_gates, dc, vp, dcp, sums, *, taps):
    total = dc.shape[0]
    last = (((1,), (1,)), ((), ()))
    full, half = slice(0, 2 * LANES), slice(2 * LANES, 3 * LANES)
    turned = lambda left, right: lax.dot_general(left, right, last, preferred_element_type=F32)

    def chunk(i, carry):
        start = pl.multiple_of(i * CHUNK, CHUNK)
        at = pl.ds(start, CHUNK)
        whole = turned(dpi[at, full], in_whole[...]) + turned(dpa[at, full], de_whole[...])
        middle = (
            turned(dpi[at, half], near_gates[:, :LANES])
            + turned(dpa[at, half], near_gates[:, LANES:])
            + turned(far[at, :], far_gates[...])
        )
        out = dc[at, :] + jnp.concatenate([whole, middle], axis=1)
        dcp[at, :] = out
        window = vp[pl.ds(start, CHUNK + 8), :]
        return tuple(
            carry[k] + jnp.sum(out * window[8 - k : 8 - k + CHUNK], axis=0, keepdims=True)
            for k in range(taps)
        )

    zero = jnp.zeros((1, dc.shape[1]), F32)
    carry = lax.fori_loop(0, total // CHUNK, chunk, (zero,) * taps)
    sums[...] = jnp.zeros_like(sums)
    for k in range(taps):
        sums[k : k + 1, :] = carry[k]


def unfilter_kernel(slot, dc, following, rows, dv, dcp, *, th, taps):
    total = dc.shape[0]
    dcp[0:total, :] = dc[...]
    dcp[total : total + 8, :] = following[...]

    def order(b, carry):
        window = dcp[pl.ds(pl.multiple_of(b * th, th), th + 8), :]
        out = rows[0:1, :] * window[0:th]
        for k in range(1, taps):
            out = out + rows[k : k + 1, :] * window[k : k + th]
        dv[pl.ds(pl.multiple_of(slot[b] * th, th), th), :] = out.astype(BF16)
        return carry

    lax.fori_loop(0, total // th, order, 0)


def feed_kernel(ge, dz, zb, dge, *, th):
    lanes = dz.shape[1]

    def block(b, carry):
        at = pl.ds(pl.multiple_of(b * th, th), th)
        g, e, d = ge[at, :lanes], ge[at, lanes:], dz[at, :]
        act, inner = gelu_parts(g)
        zb[at, :] = (act * e).astype(BF16)
        dge[at, :lanes] = (d * e * gelu_slope(g, inner)).astype(BF16)
        dge[at, lanes:] = (d * act).astype(BF16)
        return carry

    lax.fori_loop(0, dz.shape[0] // th, block, 0)


def on_chip(kernel, slot, inputs, outs, scratch=()):
    vmem = pl.BlockSpec(memory_space=pltpu.VMEM)
    return pl.pallas_call(
        kernel,
        out_shape=[jax.ShapeDtypeStruct(shape, dtype) for shape, dtype in outs],
        in_specs=[pl.BlockSpec(memory_space=pltpu.SMEM)] + [vmem] * len(inputs),
        out_specs=[vmem] * len(outs),
        scratch_shapes=[pltpu.VMEM(shape, dtype) for shape, dtype in scratch],
        compiler_params=params(),
    )(slot, *inputs)


def in_vmem(kernel, inputs, outs, scratch=()):
    vmem = pl.BlockSpec(memory_space=pltpu.VMEM)
    return pl.pallas_call(
        kernel,
        out_shape=[jax.ShapeDtypeStruct(shape, dtype) for shape, dtype in outs],
        in_specs=[vmem] * len(inputs),
        out_specs=[vmem] * len(outs),
        scratch_shapes=[pltpu.VMEM(shape, dtype) for shape, dtype in scratch],
        compiler_params=params(),
    )(*inputs)


def dot(left, right, over):
    return lax.dot_general(left, right, (over, ((), ())), preferred_element_type=F32)


def shards(
    block_input,
    first_gain,
    gelu_weight,
    scan_weight,
    filter_taps,
    input_gate,
    input_bias,
    decay_gate,
    decay_bias,
    decay_param,
    output_weight,
    second_gain,
    expand_gate,
    expand_value,
    contract_weight,
    output_cotangent,
):
    count = lax.axis_size("seq")
    chip = lax.axis_index("seq")
    core = lax.axis_index("head")
    th = block_input.shape[0] // 2
    width = block_input.shape[1]
    part = gelu_weight.shape[0]
    taps = filter_taps.shape[0]
    local_blocks, gate_rows, block_width = input_gate.shape
    assert block_width == 2 * LANES and width == part * count and local_blocks == 5
    place = chip // 4
    fours = count // 4
    near = 8 * th
    total = 2 * count * th
    lanes_r = 3 * LANES
    slab = 4 * part

    hidden = expand_gate.shape[1]
    lanes = LANES * -(-hidden // (count * LANES))
    hidden_chips = hidden // lanes
    assert hidden_chips * lanes == hidden

    number = jnp.arange(8, dtype=jnp.int32)
    relative = (chip & 3) ^ (number // 2)
    turned = ((relative & 1) << 1) | (relative >> 1)
    slot = jnp.where(number % 2 == 0, turned, relative) + jnp.where(number % 2 == core, 0, 4)
    slot = slot.astype(jnp.int32)

    def slabs(rows):
        return jnp.concatenate(
            [lax.dynamic_slice_in_dim(rows, (place ^ j) * slab, slab, 1) for j in range(fours)],
            axis=1,
        )

    extra = max(16, gate_rows)
    more_rows = ((0, 0), (0, extra - gate_rows), (0, 0))
    gain1 = first_gain.astype(F32)[:, None]
    small = jnp.concatenate(
        [
            filter_taps.transpose(1, 0, 2),
            input_bias[:, None],
            decay_bias[:, None],
            decay_param[:, None],
        ],
        axis=1,
    )
    small = jnp.pad(
        small, ((0, 0), (0, extra - small.shape[1]), (0, LANES - small.shape[2]))
    )
    packed = packed_narrow(
        gain1,
        gelu_weight,
        scan_weight,
        output_weight.T,
        jnp.pad(input_gate, more_rows),
        jnp.pad(decay_gate, more_rows),
        small,
    )

    def both_sides(pieces):
        kept = lax.dynamic_index_in_dim(pieces, core, 0, False)
        given = core_swap(lax.dynamic_index_in_dim(pieces, 1 - core, 0, False))
        return jnp.concatenate(
            [jnp.where(core == 0, kept, given), jnp.where(core == 0, given, kept)], axis=0
        )

    packed = [near_exchanged(both_sides(piece)) for piece in packed]
    pieces_yv = row_gathered(packed[0])
    weight_yv = jnp.concatenate([piece[:, 2 * extra :].reshape(slab, -1) for piece in pieces_yv])
    heads = jnp.stack([piece[:, : 2 * extra] for piece in pieces_yv])
    heads = jnp.concatenate(
        [lax.dynamic_index_in_dim(heads, place ^ j, 0, False) for j in range(fours)]
    )
    gates = heads[:, :gate_rows].reshape(block_width, 2 * lanes_r)
    small = heads[:, extra : extra + taps + 3]
    small = [
        small[:, :, i * LANES : i * LANES + gate_rows].transpose(1, 0, 2).reshape(taps + 3, -1)
        for i in range(2)
    ]
    own_half = lambda a, axis=0: lax.dynamic_slice_in_dim(a, core * LANES, LANES, axis)
    far_half = lambda a, axis=0: lax.dynamic_slice_in_dim(a, (1 - core) * LANES, LANES, axis)
    small = jnp.concatenate([small[0], own_half(small[1], 1)], axis=1).astype(F32)
    tap_rows = jnp.pad(small[:taps], ((0, 8 - taps), (0, 0)))
    param_row = small[taps + 2 :]
    gate_rows_of = jnp.pad(
        jnp.concatenate([small[taps : taps + 2], jax.nn.softplus(param_row)], axis=0),
        ((0, 5), (0, 0)),
    )
    in_whole, de_whole = gates[:, : 2 * LANES], gates[:, lanes_r : lanes_r + 2 * LANES]
    half_gates = jnp.concatenate([gates[:, 2 * LANES : lanes_r], gates[:, lanes_r + 2 * LANES :]], 1)

    x = lax.dynamic_slice_in_dim(block_input, core * th, th, 0).astype(F32)
    s1 = lax.rsqrt(jnp.mean(x * x, axis=-1, keepdims=True) + EPSILON)
    first = near_gathered(slabs((x * s1).astype(BF16)))
    cotangent = lax.dynamic_slice_in_dim(output_cotangent, core * th, th, 0)
    given_out = jnp.concatenate(gathered(after(cotangent, first)))
    pieces_out = row_gathered(after(packed[1], *pieces_yv))
    weight_out = jnp.concatenate([piece.reshape(slab, lanes_r) for piece in pieces_out])

    gain2 = second_gain.astype(F32)[:, None]
    wide = packed_wide(gain2, expand_gate, expand_value, contract_weight.T, count, lanes)
    wide = all_to_all(after(wide, weight_yv)).reshape(width, 3 * lanes)

    yv = dot(first, weight_yv, ((1,), (0,)))
    tail = lax.dynamic_slice_in_dim(yv[:, lanes_r:], slot[7] * th + th - 8, 8, 0)
    token_f32, token_bf16 = ((near, lanes_r), F32), ((near, lanes_r), BF16)
    padded = ((near + 8, lanes_r), F32)
    few = ((8, lanes_r), F32)
    tiled = ((3, near, LANES), F32)
    y, vp, c, cb = on_chip(
        functools.partial(filter_kernel, th=th, taps=taps),
        slot,
        [yv, next_four(tail, 1), tap_rows],
        [token_f32, padded, token_f32, token_bf16],
    )
    cb_far = core_swap(cb[:, 2 * LANES :])
    near_gates, far_gates = own_half(half_gates), far_half(half_gates)
    gi, ga, hp, p, ends, pair = in_vmem(
        states_kernel,
        [
            cb,
            cb_far,
            jnp.concatenate([in_whole, de_whole], axis=1),
            near_gates,
            far_gates,
            c,
            gate_rows_of,
        ],
        [token_f32, token_f32, tiled, tiled, ((16, lanes_r), F32), few],
        [tiled],
    )
    h, ob = on_chip(
        functools.partial(merge_kernel, th=th),
        slot,
        [hp, p, ends, carried(pair, place, False), y],
        [padded, token_bf16],
    )
    weight_ge, weight_c = wide[:, : 2 * lanes], wide[:, 2 * lanes :]
    dz = dot(given_out, weight_c, ((1,), (0,)))
    out_both = jnp.concatenate([weight_out, core_swap(weight_out)], axis=1)
    r = x + slabs(near_scattered(ob, out_both))

    s2 = lax.rsqrt(jnp.mean(r * r, axis=-1, keepdims=True) + EPSILON)
    second = gathered((r * s2).astype(BF16), [dz])
    second = jnp.concatenate(second)
    zb, dge = in_vmem(
        functools.partial(feed_kernel, th=th),
        [dot(second, weight_ge, ((1,), (0,))), dz],
        [((total, lanes), BF16), ((total, 2 * lanes), BF16)],
    )
    ge_both = jnp.concatenate([weight_ge, core_swap(weight_ge)], axis=1)
    c_both = jnp.concatenate([weight_c, core_swap(weight_c)], axis=1)
    (back2,) = scattered((grouped(dge), ge_both))
    dr = (
        cotangent.astype(F32)
        + s2 * back2
        - r * (s2 * s2 * s2) * jnp.mean(back2 * r, axis=-1, keepdims=True)
    )
    wide_grad, turned_grad = (
        dot(second, dge, ((0,), (0,))).astype(BF16).reshape(count, part, 2 * lanes),
        dot(given_out, zb, ((0,), (0,))).astype(BF16).reshape(count, part, lanes),
    )
    wide_grad, turned_grad = lax.optimization_barrier((wide_grad, turned_grad))
    turned_grad = all_to_all(turned_grad)
    dq = near_gathered(slabs(dr.astype(BF16)))
    dq, wide_grad = lax.optimization_barrier((dq, wide_grad))
    (out_sum,) = scattered((grouped(after(zb, dq)), c_both))
    out_half = (r + out_sum).astype(BF16)
    wide_grad = all_to_all(wide_grad)
    gate_grad_out, value_grad_out, contract_grad_out, gain2_part = unpacked_wide(
        wide_grad, turned_grad, gain2, expand_gate, expand_value, lanes
    )

    dob = dot(dq, weight_out, ((1,), (0,)))
    dy, lam, q, ends, pair = on_chip(
        functools.partial(adjoint_kernel, th=th),
        slot,
        [dob, y, h, ga, gate_rows_of],
        [token_bf16, tiled, tiled, ((16, lanes_r), F32), few],
        [tiled],
    )
    dpi, dpa, dc, sums = in_vmem(
        gates_kernel,
        [lam, q, ends, carried(pair, place, True), h, gi, ga, c, gate_rows_of],
        [token_bf16, token_bf16, token_f32, few],
    )
    half_grads = jnp.concatenate([dpi[:, 2 * LANES :], dpa[:, 2 * LANES :]], axis=1)
    dc, tap_sums = in_vmem(
        functools.partial(ungate_kernel, taps=taps),
        [
            dpi,
            dpa,
            core_swap(half_grads),
            in_whole,
            de_whole,
            near_gates,
            own_half(core_swap(half_gates)),
            dc,
            vp,
        ],
        [token_f32, few],
    )
    dv = on_chip(
        functools.partial(unfilter_kernel, th=th, taps=taps),
        slot,
        [dc, next_four(dc[:8], -1), tap_rows],
        [token_bf16],
        [padded],
    )[0]
    dyv = after(jnp.concatenate([dy, dv], axis=1), turned_grad)

    def to_owners(grad):
        grad = row_scattered(list(grad)).astype(BF16)
        grad = near_exchanged(grad)
        kept = lax.dynamic_slice_in_dim(grad, 2 * core, 2, 0)
        given = core_swap(lax.dynamic_slice_in_dim(grad, 2 * (1 - core), 2, 0))
        return jnp.stack([jnp.where(core == 0, kept, given), jnp.where(core == 0, given, kept)])

    out_grad = lax.optimization_barrier(dot(dq, ob, ((0,), (0,))).astype(BF16))
    out_grad = to_owners(out_grad.reshape(fours, 4, part, lanes_r))
    yv_grad = lax.optimization_barrier(dot(first, dyv, ((0,), (0,))).astype(BF16))
    yv_grad = yv_grad.reshape(fours, 4, part, 2 * lanes_r)

    def gate_grad(grad):
        whole = dot(cb[:, : 2 * LANES], grad[:, : 2 * LANES], ((0,), (0,)))
        own_rows = dot(cb[:, 2 * LANES :], grad[:, 2 * LANES :], ((0,), (0,)))
        far_rows = dot(cb_far, grad[:, 2 * LANES :], ((0,), (0,)))
        half = jnp.concatenate(
            [jnp.where(core == 0, own_rows, far_rows), jnp.where(core == 0, far_rows, own_rows)]
        )
        return jnp.concatenate([whole, half], axis=1)

    head_grad = jnp.concatenate([gate_grad(dpi), gate_grad(dpa)], axis=1)
    head_grad = head_grad.reshape(count, gate_rows, 2 * lanes_r)
    head_grad = jnp.pad(head_grad, ((0, 0), (0, extra - gate_rows), (0, 0)))
    small_grad = jnp.concatenate(
        [tap_sums[:taps], sums[:2], sums[2:3] * jax.nn.sigmoid(param_row)], axis=0
    )
    middle = small_grad[:, 2 * LANES :]
    nothing = jnp.zeros_like(middle)
    small_grad = [
        small_grad[:, : 2 * LANES],
        jnp.where(
            core == 0,
            jnp.concatenate([middle, nothing], axis=1),
            jnp.concatenate([nothing, middle], axis=1),
        ),
    ]
    small_grad = [
        jnp.pad(
            a.reshape(taps + 3, count, gate_rows).transpose(1, 0, 2),
            ((0, 0), (0, extra - taps - 3), (0, LANES - gate_rows)),
        )
        for a in small_grad
    ]
    small_grad = jnp.concatenate(small_grad, axis=2)
    small_grad = jnp.pad(small_grad, ((0, 0), (0, 0), (0, 2 * lanes_r - 2 * LANES)))
    head_grad = jnp.concatenate([head_grad, small_grad], axis=1).astype(BF16)
    head_grad = head_grad.reshape(fours, 4, 2 * extra, 2 * lanes_r)
    head_grad = jnp.stack(
        [lax.dynamic_index_in_dim(head_grad, place ^ j, 0, False) for j in range(fours)]
    )
    yv_grad = to_owners(jnp.concatenate([head_grad, yv_grad], axis=2))
    (
        gelu_grad_out,
        scan_grad_out,
        output_grad_out,
        input_gate_out,
        decay_gate_out,
        gain1_part,
    ) = unpacked_narrow(
        yv_grad, out_grad, gain1, gelu_weight, scan_weight, local_blocks, gate_rows, extra
    )
    small_sum = yv_grad[:, :, extra : extra + taps + 3].astype(F32)
    whole_sum = small_sum[..., :gate_rows]
    half_sum = small_sum[..., LANES : LANES + gate_rows]
    half_sum = half_sum[0] + half_sum[1]
    small_sum = jnp.stack(
        [whole_sum[0, 0], half_sum[0], whole_sum[1, 0], whole_sum[0, 1], whole_sum[1, 1]], axis=1
    )

    back1 = slabs(near_scattered(dyv, weight_yv, core_swap(weight_yv)))
    in_half = dr + s1 * back1 - x * (s1 * s1 * s1) * jnp.mean(back1 * x, axis=-1, keepdims=True)

    gain_parts = jnp.stack([jnp.sum(gain1_part, axis=1), jnp.sum(gain2_part, axis=1)])
    gain_grads = gain_parts + core_swap(gain_parts)

    def both_halves(half):
        swapped = core_swap(half)
        return jnp.concatenate(
            [jnp.where(core == 0, half, swapped), jnp.where(core == 0, swapped, half)], axis=0
        )

    return (
        both_halves(out_half),
        both_halves(in_half),
        gain_grads[0],
        gelu_grad_out,
        scan_grad_out,
        small_sum[:taps],
        input_gate_out,
        small_sum[taps],
        decay_gate_out,
        small_sum[taps + 1],
        small_sum[taps + 2],
        output_grad_out.T,
        gain_grads[1],
        gate_grad_out,
        value_grad_out,
        contract_grad_out.T,
    )


def solution(mesh):
    in_specs = (
        P("seq", None),
        P("seq"),
        P("seq", "head"),
        P("seq", "head"),
        P(None, "head", "seq"),
        P("head", "seq", None),
        P("head", "seq"),
        P("head", "seq", None),
        P("head", "seq"),
        P("head", "seq"),
        P("head", "seq"),
        P("seq"),
        P("seq", "head"),
        P("seq", "head"),
        P("head", "seq"),
        P("seq", None),
    )
    out_specs = (
        P("seq", None),
        P("seq", None),
        P("seq"),
        P("seq", "head"),
        P("seq", "head"),
        P(None, "head", "seq"),
        P("head", "seq", None),
        P("head", "seq"),
        P("head", "seq", None),
        P("head", "seq"),
        P("head", "seq"),
        P("head", "seq"),
        P("seq"),
        P("seq", "head"),
        P("seq", "head"),
        P("head", "seq"),
    )
    return jax.shard_map(shards, mesh=mesh, in_specs=in_specs, out_specs=out_specs, check_vma=False)
```
